512 devices in a mesh: lat: 16 (over z_lo, core), lon: 32 (over x, y, z_hi).
Axes of the slice: x: 4, y: 4, z: 16 (z_hi: 2, z_lo: 8; z = z_hi * 8 + z_lo), core: 2. Of those that a mesh axis runs over, the one named last changes fastest.
Arguments:
- student: bfloat16 [2, 64, 1024, 256], P(None, 'lat', 'lon'), may hold values from -6 to 6
- teacher: bfloat16 [2, 64, 1024, 256], P(None, None, ('lon', 'lat')), may hold values from -6 to 6
- dw_weight: float32 [7, 7, 256], replicated, may hold values from -0.875 to 0.875
- norm_gain: float32 [256], replicated, may hold values from 0.1 to 1.9
- w_in: bfloat16 [256, 1024], replicated, may hold values from -0.375 to 0.375
- w_out: bfloat16 [1024, 256], replicated, may hold values from -0.1875 to 0.1875
- layer_scale: float32 [256], replicated, may hold values from 0.3 to 1.5
Outputs:
- grad_student: bfloat16 [2, 64, 1024, 256], P(None, 'lat', 'lon')
- grad_w_in: float32 [256, 1024], replicated
- grad_w_out: float32 [1024, 256], replicated
- grad_dw: float32 [7, 7, 256], replicated
The draws below stay inside these ranges and needn't reach their ends.
All inputs are finite; a program needn't handle non-finite values.
Results may differ from the reference program's by a relative error of at most 0.0034.
The reference program's roundings to bfloat16 on the way (of `normed`, `hidden`, `out_grad`, `preact_grad` and `conv_grad`) count: a program that leaves them out, or rounds other values in their place, can miss the bound.
Values may be sent and summed in bfloat16 or wider, within the bound.
A program may use at most 64 MiB of HBM per device.

```python
import math
import jax
import jax.numpy as jnp
from jax import lax

BATCH = 2
CHANNELS = 256
HIDDEN_SIZE = 1024
KERNEL = 7
NLAT = 64
NLON = 1024
CELLS = 131072


def block_levels(stream_key, shape, cuts, least, top_value):
    factor_of = 1.0
    for position, shards_of in cuts:
        steps = jax.random.uniform(jax.random.fold_in(jax.random.fold_in(stream_key, 6), position), (shards_of,), jnp.float32, least / len(cuts), top_value / len(cuts))
        factor_of = factor_of * jnp.repeat(jnp.exp(steps), shape[position] // shards_of).reshape((-1,) + (1,) * (len(shape) - 1 - position))
    return factor_of


def noise(rng, extent, scale, most, cuts=(), held_as=jnp.bfloat16):
    values = jax.random.normal(rng, extent, jnp.float32) * scale
    if len(cuts) > 0:
        values = block_levels(rng, extent, cuts, -0.22, 0.18) * values
    return jnp.clip(values, min=-most, max=most).astype(held_as)


def setup_inputs(seed: int = 0) -> dict:
    key_of = jax.random.split(jax.random.key(seed), 8)
    student = noise(key_of[0], (BATCH, NLAT, NLON, CHANNELS), 1.0, 6.0, ((1, 16), (2, 32)))
    teacher = noise(key_of[1], (BATCH, NLAT, NLON, CHANNELS), 1.0, 6.0, ((2, 512),))
    dw_weight = noise(key_of[2], (KERNEL, KERNEL, CHANNELS), (KERNEL * KERNEL) ** -0.5, 0.875, (), jnp.float32)
    norm_gain = jnp.clip(1.0 + 0.18 * jax.random.normal(key_of[3], (CHANNELS,), jnp.float32), 0.1, 1.9)
    w_in = noise(key_of[4], (CHANNELS, HIDDEN_SIZE), CHANNELS ** -0.5, 0.375)
    w_out = noise(key_of[5], (HIDDEN_SIZE, CHANNELS), HIDDEN_SIZE ** -0.5, 0.1875)
    layer_scale = jnp.clip(jnp.exp(jax.random.uniform(key_of[6], (CHANNELS,), jnp.float32, math.log(0.3), math.log(1.5))), 0.3, 1.5)
    return dict(student=student, teacher=teacher, dw_weight=dw_weight, norm_gain=norm_gain, w_in=w_in, w_out=w_out, layer_scale=layer_scale)


slope_coef = 0.7978845608028654
cubic_coef = 0.044715
norm_eps = 1e-06

def gelu_tanh(values):
    tanh_arg = slope_coef * (values + cubic_coef * values * values * values)
    return 0.5 * values * (1.0 + jnp.tanh(tanh_arg))

def gelu_slope(values):
    tangent = jnp.tanh(slope_coef * (values + cubic_coef * values * values * values))
    return 0.5 * (1.0 + tangent) + 0.5 * values * (1.0 - tangent * tangent) * slope_coef * (1.0 + 3.0 * cubic_coef * values * values)

def forward_cells(smoothed, student_rows, norm_gain, w_in, w_out, layer_scale):
    average = lax.optimization_barrier(jnp.mean(smoothed, axis=-1, keepdims=True))
    centred = smoothed - average
    variance = lax.optimization_barrier(jnp.mean(centred * centred, axis=-1, keepdims=True))
    inv_std = lax.rsqrt(variance + norm_eps)
    unit_norm = centred * inv_std
    normed = (unit_norm * norm_gain).astype(jnp.bfloat16)
    preact = jnp.dot(normed, w_in, preferred_element_type=jnp.float32)
    hidden = gelu_tanh(preact).astype(jnp.bfloat16)
    mlp_out = jnp.dot(hidden, w_out, preferred_element_type=jnp.float32)
    output = student_rows.astype(jnp.float32) + layer_scale * mlp_out
    return (output, (normed, unit_norm, inv_std, preact, hidden))

def backward_cells(misfit, stored, norm_gain, w_in, w_out, layer_scale):
    normed, unit_norm, inv_std, preact, hidden = stored
    out_grad = (layer_scale * misfit).astype(jnp.bfloat16)
    part_out = lax.dot_general(hidden, out_grad, (((0,), (0,)), ((), ())), preferred_element_type=jnp.float32)
    hidden_grad = lax.dot_general(out_grad, w_out, (((1,), (1,)), ((), ())), preferred_element_type=jnp.float32)
    preact_grad = (hidden_grad * gelu_slope(preact)).astype(jnp.bfloat16)
    part_in = lax.dot_general(normed, preact_grad, (((0,), (0,)), ((), ())), preferred_element_type=jnp.float32)
    normed_grad = lax.dot_general(preact_grad, w_in, (((1,), (1,)), ((), ())), preferred_element_type=jnp.float32)
    unit_grad = normed_grad * norm_gain
    first_mean = lax.optimization_barrier(jnp.mean(unit_grad, axis=-1, keepdims=True))
    second_mean = lax.optimization_barrier(jnp.mean(unit_grad * unit_norm, axis=-1, keepdims=True))
    conv_grad = inv_std * (unit_grad - first_mean - unit_norm * second_mean)
    return (conv_grad.astype(jnp.bfloat16), part_in, part_out)

def extend_grid(field):
    half_kernel = KERNEL // 2
    lon_padded = jnp.concatenate([field[:, :, NLON - half_kernel:], field, field[:, :, :half_kernel]], axis=2)
    lon_padded = lon_padded.astype(jnp.float32)
    return jnp.pad(lon_padded, ((0, 0), (half_kernel, half_kernel), (0, 0), (0, 0)))

def reference(student, teacher, dw_weight, norm_gain, w_in, w_out, layer_scale):
    padded = extend_grid(student)
    smoothed = jnp.zeros((BATCH, NLAT, NLON, CHANNELS), jnp.float32)
    for row_off in range(KERNEL):
        for col_off in range(KERNEL):
            smoothed = smoothed + dw_weight[row_off, col_off] * padded[:, row_off:row_off + NLAT, col_off:col_off + NLON]

    def one_line(totals, pieces):
        smooth_line, student_line, teacher_line = pieces
        output, stored = forward_cells(smooth_line, student_line, norm_gain, w_in, w_out, layer_scale)
        misfit = output - teacher_line.astype(jnp.float32)
        conv_grad, part_in, part_out = backward_cells(misfit, stored, norm_gain, w_in, w_out, layer_scale)
        return ((totals[0] + part_in, totals[1] + part_out), (conv_grad, misfit))
    start_totals = (jnp.zeros((CHANNELS, HIDDEN_SIZE), jnp.float32), jnp.zeros((HIDDEN_SIZE, CHANNELS), jnp.float32))
    line_inputs = (smoothed.reshape(BATCH * NLAT, NLON, CHANNELS), student.reshape(BATCH * NLAT, NLON, CHANNELS), teacher.reshape(BATCH * NLAT, NLON, CHANNELS))
    (sum_in, sum_out), (conv_grad, misfit) = lax.scan(one_line, start_totals, line_inputs)
    conv_grad = conv_grad.reshape(BATCH, NLAT, NLON, CHANNELS)
    misfit = misfit.reshape(BATCH, NLAT, NLON, CHANNELS)
    padded_grad = extend_grid(conv_grad)
    conv_grad_f = conv_grad.astype(jnp.float32)
    back_conv = jnp.zeros((BATCH, NLAT, NLON, CHANNELS), jnp.float32)
    kernel_terms = []
    for row_off in range(KERNEL):
        for col_off in range(KERNEL):
            row_start = KERNEL - 1 - row_off
            col_start = KERNEL - 1 - col_off
            back_conv = back_conv + dw_weight[row_off, col_off] * padded_grad[:, row_start:row_start + NLAT, col_start:col_start + NLON]
            kernel_terms.append(lax.optimization_barrier(jnp.sum(padded[:, row_off:row_off + NLAT, col_off:col_off + NLON] * conv_grad_f, axis=(0, 1, 2))))
    grad_student = (misfit + back_conv).astype(jnp.bfloat16)
    grad_dw = jnp.stack(kernel_terms).reshape(KERNEL, KERNEL, CHANNELS) / CELLS
    return (grad_student, sum_in / CELLS, sum_out / CELLS, grad_dw)
```

```python
import jax
import jax.numpy as jnp
from jax import lax
from jax.experimental import pallas as pl
from jax.experimental.pallas import tpu as pltpu
from jax.sharding import PartitionSpec as P

slope_coef = 0.7978845608028654
cubic_coef = 0.044715
norm_eps = 1e-06
MESH = pl.DeviceIdType.MESH

BLOCKS, SIDE, SPLIT, TILE, DW_ROWS, DW_PAD = 16, 128, 64, 8, 4, 16
LOWER = SIDE - SPLIT + DW_PAD
CHIPS_Z = 16


def sum_kernel(
    left_a, right_a, left_b, right_b, dw_ref, out_a, out_b, out_dw,
    own, other, dw_other, top, low, top_in1, low_in1, top1, low1, top_in2, low_in2,
    z_send, z_in, z_own, z_all, top_g1, low_g1, top_all, low_all,
    core_ssem, core_rsem, xy_ssem, xy_rsem, z_ssem, z_rsem,
):
    lat, lon = lax.axis_index("lat"), lax.axis_index("lon")
    core = lax.rem(lat, 2)
    z = lax.rem(lon, 2) * 8 + lat // 2
    x = lon // 8
    y = lax.rem(lon // 2, 4)

    def device(core_to, z_to, x_to, y_to):
        return {
            "lat": lax.rem(z_to, 8) * 2 + core_to,
            "lon": x_to * 8 + y_to * 2 + z_to // 8,
        }

    partner = device(1 - core, z, x, y)
    x_peers = [lax.rem(x + d, 4) for d in range(4)]
    y_peers = [lax.rem(y + d, 4) for d in range(4)]
    z_peers = [lax.rem(z + d, CHIPS_Z) for d in range(CHIPS_Z)]
    x_devices = [device(core, z, p, y) for p in x_peers]
    y_devices = [device(core, z, x, p) for p in y_peers]
    z_devices = [device(core, p, x, y) for p in z_peers]

    barrier = pltpu.get_barrier_semaphore()
    friends = [partner] + x_devices[1:] + y_devices[1:] + z_devices[1:]
    for friend in friends:
        pl.semaphore_signal(barrier, inc=1, device_id=friend, device_id_type=MESH)

    def send(source, target, ssem, rsem, device_to):
        copy = pltpu.make_async_remote_copy(
            src_ref=source, dst_ref=target, send_sem=ssem, recv_sem=rsem,
            device_id=device_to, device_id_type=MESH,
        )
        copy.start()
        return copy

    for which, (left, right) in enumerate(((left_a, right_a), (left_b, right_b))):
        product = lax.dot_general(
            left[...], right[...], (((0,), (0,)), ((), ())), preferred_element_type=jnp.float32
        )
        for block in range(BLOCKS):
            row, col = SIDE * (block // 8), SIDE * (block % 8)
            own[which, block] = product[row : row + SIDE, col : col + SIDE]
    pl.semaphore_wait(barrier, len(friends))

    copies = [
        send(own.at[1 - core], other, core_ssem.at[0], core_rsem.at[0], partner),
        send(dw_ref.at[1 - core], dw_other, core_ssem.at[1], core_rsem.at[1], partner),
    ]
    for copy in copies:
        copy.wait()
    for block in range(BLOCKS):
        bx, by = block // 4, block % 4
        top[bx, by] = own[core, block, :SPLIT] + other[block, :SPLIT]
        low[by, bx, : SIDE - SPLIT] = own[core, block, SPLIT:] + other[block, SPLIT:]
        rows = slice(DW_ROWS * block, DW_ROWS * (block + 1))
        dw_sum = dw_ref[core, rows] + dw_other[rows]
        low[by, bx, SIDE - SPLIT :] = jnp.concatenate(
            [dw_sum, jnp.zeros((DW_PAD - DW_ROWS, SIDE), jnp.float32)], axis=0
        )

    copies = []
    for d in (2, 1, 3):
        copies.append(
            send(top.at[x_peers[d]], top_in1.at[d], xy_ssem.at[0, d], xy_rsem.at[0, d], x_devices[d])
        )
        copies.append(
            send(low.at[y_peers[d]], low_in1.at[d], xy_ssem.at[1, d], xy_rsem.at[1, d], y_devices[d])
        )
    for copy in copies:
        copy.wait()
    top1[...] = top[x] + top_in1[1] + top_in1[2] + top_in1[3]
    low1[...] = low[y] + low_in1[1] + low_in1[2] + low_in1[3]

    copies = []
    for d in (2, 1, 3):
        copies.append(
            send(top1.at[y_peers[d]], top_in2.at[d], xy_ssem.at[2, d], xy_rsem.at[2, d], y_devices[d])
        )
        copies.append(
            send(low1.at[x_peers[d]], low_in2.at[d], xy_ssem.at[3, d], xy_rsem.at[3, d], x_devices[d])
        )
    for copy in copies:
        copy.wait()
    top2 = top1[y] + top_in2[1] + top_in2[2] + top_in2[3]
    low2 = low1[x] + low_in2[1] + low_in2[2] + low_in2[3]
    for tile in range(CHIPS_Z):
        at = TILE * tile
        z_send[tile, :TILE] = top2[at : at + TILE] if at < SPLIT else low2[at - SPLIT : at - SPLIT + TILE]
        z_send[tile, TILE:] = low2[SIDE - SPLIT : SIDE - SPLIT + TILE]

    order = [8, 7, 9, 6, 10, 5, 11, 4, 12, 3, 13, 2, 14, 1, 15]
    copies = []
    for d in order:
        copies.append(
            send(z_send.at[z_peers[d]], z_in.at[z], z_ssem.at[0, d], z_rsem.at[0, d], z_devices[d])
        )
    z_in[z] = z_send[z]
    for copy in copies:
        copy.wait()
    total = z_in[0]
    for tile in range(1, CHIPS_Z):
        total = total + z_in[tile]
    z_own[...] = total

    copies = []
    for d in order:
        copies.append(
            send(z_own.at[:TILE], z_all.at[z], z_ssem.at[1, d], z_rsem.at[1, d], z_devices[d])
        )
    z_all[z] = z_own[:TILE]
    for copy in copies:
        copy.wait()
    tiles = z_all[...].reshape(SIDE, SIDE)
    dw_tile = jnp.concatenate(
        [z_own[TILE:], jnp.zeros((DW_PAD - TILE, SIDE), jnp.float32)], axis=0
    )
    top_g1[y] = tiles[:SPLIT].astype(jnp.bfloat16)
    low_g1[x] = jnp.concatenate([tiles[SPLIT:], dw_tile], axis=0).astype(jnp.bfloat16)

    copies = []
    for d in (2, 1, 3):
        copies.append(
            send(top_g1.at[y], top_g1.at[y], xy_ssem.at[4, d], xy_rsem.at[4, d], y_devices[d])
        )
        copies.append(
            send(low_g1.at[x], low_g1.at[x], xy_ssem.at[5, d], xy_rsem.at[5, d], x_devices[d])
        )
    for copy in copies:
        copy.wait()

    copies = []
    for d in (2, 1, 3):
        copies.append(
            send(top_g1, top_all.at[core, x], xy_ssem.at[6, d], xy_rsem.at[6, d], x_devices[d])
        )
        copies.append(
            send(low_g1, low_all.at[core, y], xy_ssem.at[7, d], xy_rsem.at[7, d], y_devices[d])
        )
    top_all[core, x] = top_g1[...]
    low_all[core, y] = low_g1[...]
    for copy in copies:
        copy.wait()

    copies = [
        send(top_all.at[core], top_all.at[core], core_ssem.at[2], core_rsem.at[2], partner),
        send(low_all.at[core], low_all.at[core], core_ssem.at[3], core_rsem.at[3], partner),
    ]
    for copy in copies:
        copy.wait()
    for which, out in enumerate((out_a, out_b)):
        for block in range(BLOCKS):
            bx, by = block // 4, block % 4
            row, col = SIDE * (block // 8), SIDE * (block % 8)
            out[row : row + SPLIT, col : col + SIDE] = top_all[which, bx, by]
            out[row + SPLIT : row + SIDE, col : col + SIDE] = low_all[which, by, bx, : SIDE - SPLIT]
            dw_rows = low_all[which, by, bx, SIDE - SPLIT :].astype(jnp.float32)[:DW_ROWS]
            out_dw[which, DW_ROWS * block : DW_ROWS * (block + 1)] = dw_rows


def sum_gradients(left_a, right_a, left_b, right_b, dw):
    f32, bf16 = jnp.float32, jnp.bfloat16
    vmem = pl.BlockSpec(memory_space=pltpu.VMEM)
    shape = (left_a.shape[1], right_a.shape[1])
    return pl.pallas_call(
        sum_kernel,
        out_shape=(
            jax.ShapeDtypeStruct(shape, bf16),
            jax.ShapeDtypeStruct(shape, bf16),
            jax.ShapeDtypeStruct(dw.shape, f32),
        ),
        in_specs=[vmem] * 5,
        out_specs=(vmem,) * 3,
        scratch_shapes=[
            pltpu.VMEM((2, BLOCKS, SIDE, SIDE), f32),
            pltpu.VMEM((BLOCKS, SIDE, SIDE), f32),
            pltpu.VMEM(dw.shape[1:], f32),
            pltpu.VMEM((4, 4, SPLIT, SIDE), f32),
            pltpu.VMEM((4, 4, LOWER, SIDE), f32),
            pltpu.VMEM((4, 4, SPLIT, SIDE), f32),
            pltpu.VMEM((4, 4, LOWER, SIDE), f32),
            pltpu.VMEM((4, SPLIT, SIDE), f32),
            pltpu.VMEM((4, LOWER, SIDE), f32),
            pltpu.VMEM((4, SPLIT, SIDE), f32),
            pltpu.VMEM((4, LOWER, SIDE), f32),
            pltpu.VMEM((CHIPS_Z, 2 * TILE, SIDE), f32),
            pltpu.VMEM((CHIPS_Z, 2 * TILE, SIDE), f32),
            pltpu.VMEM((2 * TILE, SIDE), f32),
            pltpu.VMEM((CHIPS_Z, TILE, SIDE), f32),
            pltpu.VMEM((4, SPLIT, SIDE), bf16),
            pltpu.VMEM((4, LOWER, SIDE), bf16),
            pltpu.VMEM((2, 4, 4, SPLIT, SIDE), bf16),
            pltpu.VMEM((2, 4, 4, LOWER, SIDE), bf16),
            pltpu.SemaphoreType.DMA((4,)),
            pltpu.SemaphoreType.DMA((4,)),
            pltpu.SemaphoreType.DMA((8, 4)),
            pltpu.SemaphoreType.DMA((8, 4)),
            pltpu.SemaphoreType.DMA((2, CHIPS_Z)),
            pltpu.SemaphoreType.DMA((2, CHIPS_Z)),
        ],
        compiler_params=pltpu.CompilerParams(collective_id=0, has_side_effects=True),
    )(left_a, right_a, left_b, right_b, dw)


def with_halo(block, sides, width, periodic):
    for axis, dim in sides:
        count = lax.axis_size(axis)
        forward = [(i, i + 1) for i in range(count - 1)]
        if periodic:
            forward.append((count - 1, 0))
        backward = [(target, source) for source, target in forward]
        low = lax.ppermute(
            lax.slice_in_dim(block, block.shape[dim] - width, None, axis=dim), axis, forward
        )
        high = lax.ppermute(lax.slice_in_dim(block, 0, width, axis=dim), axis, backward)
        block = jnp.concatenate([low, block, high], axis=dim)
    return block


def gelu_tanh(values):
    tanh_arg = slope_coef * (values + cubic_coef * values * values * values)
    return 0.5 * values * (1.0 + jnp.tanh(tanh_arg))


def gelu_slope(values):
    tangent = jnp.tanh(slope_coef * (values + cubic_coef * values * values * values))
    return 0.5 * (1.0 + tangent) + 0.5 * values * (1.0 - tangent * tangent) * slope_coef * (
        1.0 + 3.0 * cubic_coef * values * values
    )


def apply_stencil(padded, dw_weight, tile_rows, tile_cols, flipped):
    kernel_size = dw_weight.shape[0]
    result = jnp.zeros((padded.shape[0], tile_rows, tile_cols, padded.shape[3]), jnp.float32)
    for row_off in range(kernel_size):
        for col_off in range(kernel_size):
            row_start = kernel_size - 1 - row_off if flipped else row_off
            col_start = kernel_size - 1 - col_off if flipped else col_off
            result = (
                result
                + dw_weight[row_off, col_off]
                * padded[:, row_start : row_start + tile_rows, col_start : col_start + tile_cols]
            )
    return result


def local(student, teacher, dw_weight, norm_gain, w_in, w_out, layer_scale):
    batch_size, tile_rows, tile_cols, channel_count = student.shape
    kernel_size = dw_weight.shape[0]
    half_kernel = kernel_size // 2
    cell_total = batch_size * tile_rows * lax.axis_size("lat") * tile_cols * lax.axis_size("lon")
    lon_padded = with_halo(student, (("lon", 2),), half_kernel, True)
    padded_bf = with_halo(lon_padded, (("lat", 1),), half_kernel, False)
    padded = padded_bf.astype(jnp.float32)
    smoothed = apply_stencil(padded, dw_weight, tile_rows, tile_cols, False).reshape(
        -1, channel_count
    )
    average = jnp.mean(smoothed, axis=-1, keepdims=True)
    centred = smoothed - average
    variance = jnp.mean(centred * centred, axis=-1, keepdims=True)
    inv_std = lax.rsqrt(variance + norm_eps)
    unit_norm = centred * inv_std
    normed = (unit_norm * norm_gain).astype(jnp.bfloat16)
    preact = jnp.dot(normed, w_in, preferred_element_type=jnp.float32)
    hidden = gelu_tanh(preact).astype(jnp.bfloat16)
    mlp_out = jnp.dot(hidden, w_out, preferred_element_type=jnp.float32)
    output = student.reshape(-1, channel_count).astype(jnp.float32) + layer_scale * mlp_out
    target = lax.all_to_all(teacher, "lat", split_axis=1, concat_axis=2, tiled=True)
    misfit = output - target.reshape(-1, channel_count).astype(jnp.float32)
    out_grad = (layer_scale * misfit).astype(jnp.bfloat16)
    hidden_grad = lax.dot_general(
        out_grad, w_out, (((1,), (1,)), ((), ())), preferred_element_type=jnp.float32
    )
    preact_grad = (hidden_grad * gelu_slope(preact)).astype(jnp.bfloat16)
    normed_grad = lax.dot_general(
        preact_grad, w_in, (((1,), (1,)), ((), ())), preferred_element_type=jnp.float32
    )
    unit_grad = normed_grad * norm_gain
    first_mean = jnp.mean(unit_grad, axis=-1, keepdims=True)
    second_mean = jnp.mean(unit_grad * unit_norm, axis=-1, keepdims=True)
    conv_grad = (inv_std * (unit_grad - first_mean - unit_norm * second_mean)).astype(jnp.bfloat16)
    conv_grid = conv_grad.reshape(student.shape)
    grad_lon = with_halo(conv_grid, (("lon", 2),), half_kernel, True)
    padded_grad = with_halo(grad_lon, (("lat", 1),), half_kernel, False).astype(jnp.float32)
    back_conv = apply_stencil(padded_grad, dw_weight, tile_rows, tile_cols, True)
    grad_student = (misfit.reshape(student.shape) + back_conv).astype(jnp.bfloat16)
    conv_grad_f = conv_grid.astype(jnp.float32)
    kernel_terms = []
    for row_off in range(kernel_size):
        for col_off in range(kernel_size):
            kernel_terms.append(
                jnp.sum(
                    padded[:, row_off : row_off + tile_rows, col_off : col_off + tile_cols]
                    * conv_grad_f,
                    axis=(0, 1, 2),
                )
            )
    taps = kernel_size * kernel_size
    part_dw = jnp.pad(jnp.stack(kernel_terms), ((0, BLOCKS * DW_ROWS - taps), (0, 0)))
    part_dw = part_dw.reshape(BLOCKS * DW_ROWS, 2, SIDE).transpose(1, 0, 2)
    sum_in, sum_out, sum_dw = sum_gradients(normed, preact_grad, out_grad, hidden, part_dw)
    sum_dw = sum_dw.transpose(1, 0, 2)[:taps].reshape(kernel_size, kernel_size, channel_count)
    return (
        grad_student,
        sum_in.astype(jnp.float32) / cell_total,
        sum_out.T.astype(jnp.float32) / cell_total,
        sum_dw / cell_total,
    )


def solution(mesh):
    placed = (
        P(None, "lat", "lon", None),
        P(None, None, ("lon", "lat"), None),
        P(),
        P(),
        P(),
        P(),
        P(),
    )
    return jax.shard_map(
        local,
        mesh=mesh,
        in_specs=placed,
        out_specs=(P(None, "lat", "lon", None), P(), P(), P()),
        check_vma=False,
    )
```

```python
import jax
import jax.numpy as jnp
from jax import lax
from jax.experimental import pallas as pl
from jax.experimental.pallas import tpu as pltpu
from jax.sharding import PartitionSpec as P

slope_coef = 0.7978845608028654
cubic_coef = 0.044715
norm_eps = 1e-06
MESH = pl.DeviceIdType.MESH

def start_remote(source, target, ssem, rsem, device_to):
    copy = pltpu.make_async_remote_copy(
        src_ref=source, dst_ref=target, send_sem=ssem, recv_sem=rsem,
        device_id=device_to, device_id_type=MESH,
    )
    copy.start()
    return copy


DIRECTIONS = [(0, 1), (0, -1), (1, 1), (1, -1), (-1, 1), (-1, -1), (1, 0), (-1, 0)]
WIDTH = 3


def halo_friends(lat, lon, lats, lons):
    return [
        {"lat": lax.rem(lat + dl + lats, lats), "lon": lax.rem(lon + dn + lons, lons)}
        for dl, dn in DIRECTIONS
    ]


def halo_copies(block, edges, low, high, left, right, ssem, rsem):
    lats, lons = lax.axis_size("lat"), lax.axis_size("lon")
    lat, lon = lax.axis_index("lat"), lax.axis_index("lon")
    rows = block.shape[1]
    copies = []
    for k, (dl, dn) in enumerate(DIRECTIONS):
        if dl == 0:
            src_rows, dst_rows = pl.ds(0, rows), pl.ds(WIDTH, rows)
        elif dl > 0:
            src_rows, dst_rows = pl.ds(rows - WIDTH, WIDTH), pl.ds(0, WIDTH)
        else:
            src_rows, dst_rows = pl.ds(0, WIDTH), pl.ds(WIDTH + rows, WIDTH)
        if dn == 0:
            source, target = block.at[:, src_rows], (low if dl > 0 else high)
        elif dn > 0:
            source, target = edges.at[1, src_rows], left.at[dst_rows]
        else:
            source, target = edges.at[0, src_rows], right.at[dst_rows]
        copy = pltpu.make_async_remote_copy(
            src_ref=source, dst_ref=target, send_sem=ssem.at[k], recv_sem=rsem.at[k],
            device_id={
                "lat": jnp.clip(lat + dl, 0, lats - 1),
                "lon": lax.rem(lon + dn + lons, lons),
            },
            device_id_type=MESH,
        )
        if dl == 0:
            sends = comes = None
        elif dl > 0:
            sends, comes = lat < lats - 1, lat > 0
        else:
            sends, comes = lat > 0, lat < lats - 1
        copies.append((copy, sends, comes))
    return copies


def run_if(condition, action):
    if condition is None:
        action()
    else:
        pl.when(condition)(action)


def halo_start(copies, low, high, left, right):
    lats, lat = lax.axis_size("lat"), lax.axis_index("lat")
    for copy, sends, _ in copies:
        run_if(sends, copy.start)
    rows = left.shape[0]

    @pl.when(lat == 0)
    def _():
        low[...] = jnp.zeros_like(low)
        left[:WIDTH] = jnp.zeros((WIDTH,) + left.shape[1:], left.dtype)
        right[:WIDTH] = jnp.zeros((WIDTH,) + right.shape[1:], right.dtype)

    @pl.when(lat == lats - 1)
    def _():
        high[...] = jnp.zeros_like(high)
        left[rows - WIDTH :] = jnp.zeros((WIDTH,) + left.shape[1:], left.dtype)
        right[rows - WIDTH :] = jnp.zeros((WIDTH,) + right.shape[1:], right.dtype)


def halo_wait(copies):
    for copy, sends, comes in copies:
        run_if(sends, copy.wait_send)
        run_if(comes, copy.wait_recv)


def halo_shapes(block):
    batch, rows, cols, channels = block.shape
    across = jax.ShapeDtypeStruct((batch, WIDTH, cols, channels), block.dtype)
    along = jax.ShapeDtypeStruct((rows + 2 * WIDTH, batch * WIDTH, channels), block.dtype)
    return (across, across, along, along)


def pack_edges(block):
    batch, rows, cols, channels = block.shape
    sides = jnp.stack([block[:, :, :WIDTH], block[:, :, cols - WIDTH :]])
    return sides.transpose(0, 2, 1, 3, 4).reshape(2, rows, batch * WIDTH, channels)


def join_halo(block, low, high, left, right):
    batch, rows, cols, channels = block.shape

    def columns(side):
        return side.reshape(rows + 2 * WIDTH, batch, WIDTH, channels).transpose(1, 0, 2, 3)

    middle = jnp.concatenate([low, block, high], axis=1)
    return jnp.concatenate([columns(left), middle, columns(right)], axis=2)


def front_kernel(
    block, edges, sent, low, high, left, right, came, halo_ssem, halo_rsem, ssem, rsem, local_sem
):
    lats, lons = lax.axis_size("lat"), lax.axis_size("lon")
    lat, lon = lax.axis_index("lat"), lax.axis_index("lon")
    peers = [lax.rem(lat + d, lats) for d in range(lats)]
    friends = halo_friends(lat, lon, lats, lons)[:6] + [{"lat": p, "lon": lon} for p in peers[1:]]
    barrier = pltpu.get_barrier_semaphore()
    for friend in friends:
        pl.semaphore_signal(barrier, inc=1, device_id=friend, device_id_type=MESH)
    mine = pltpu.make_async_copy(sent.at[lat], came.at[lat], local_sem)
    mine.start()
    pl.semaphore_wait(barrier, len(friends))
    halo = halo_copies(block, edges, low, high, left, right, halo_ssem, halo_rsem)
    halo_start(halo, low, high, left, right)
    copies = [
        start_remote(
            sent.at[peers[d]], came.at[lat], ssem.at[d], rsem.at[d], {"lat": peers[d], "lon": lon}
        )
        for d in range(1, lats)
    ]
    halo_wait(halo)
    mine.wait()
    for copy in copies:
        copy.wait()


def front_exchange(block, edges, sent):
    vmem = pl.BlockSpec(memory_space=pltpu.VMEM)
    lats = sent.shape[0]
    return pl.pallas_call(
        front_kernel,
        out_shape=halo_shapes(block) + (jax.ShapeDtypeStruct(sent.shape, sent.dtype),),
        in_specs=[vmem] * 3,
        out_specs=(vmem,) * 5,
        scratch_shapes=[
            pltpu.SemaphoreType.DMA((8,)),
            pltpu.SemaphoreType.DMA((8,)),
            pltpu.SemaphoreType.DMA((lats,)),
            pltpu.SemaphoreType.DMA((lats,)),
            pltpu.SemaphoreType.DMA,
        ],
        compiler_params=pltpu.CompilerParams(collective_id=1, has_side_effects=True),
    )(block, edges, sent)


BLOCKS, SIDE, SPLIT, TILE, DW_ROWS, DW_PAD = 16, 128, 64, 8, 4, 16
LOWER = SIDE - SPLIT + DW_PAD
CHIPS_Z = 16


def sum_kernel(
    left_a, right_a, left_b, right_b, dw_ref, block_ref, edges,
    out_a, out_b, out_dw, halo_low, halo_high, halo_left, halo_right,
    own, other, dw_other, top, low, top_in1, low_in1, top1, low1, top_in2, low_in2,
    z_send, z_in, z_own, z_all, top_g1, low_g1, top_all, low_all,
    core_ssem, core_rsem, xy_ssem, xy_rsem, z_ssem, z_rsem, halo_ssem, halo_rsem,
):
    lat, lon = lax.axis_index("lat"), lax.axis_index("lon")
    core = lax.rem(lat, 2)
    z = lax.rem(lon, 2) * 8 + lat // 2
    x = lon // 8
    y = lax.rem(lon // 2, 4)

    def device(core_to, z_to, x_to, y_to):
        return {
            "lat": lax.rem(z_to, 8) * 2 + core_to,
            "lon": x_to * 8 + y_to * 2 + z_to // 8,
        }

    partner = device(1 - core, z, x, y)
    x_peers = [lax.rem(x + d, 4) for d in range(4)]
    y_peers = [lax.rem(y + d, 4) for d in range(4)]
    z_peers = [lax.rem(z + d, CHIPS_Z) for d in range(CHIPS_Z)]
    x_devices = [device(core, z, p, y) for p in x_peers]
    y_devices = [device(core, z, x, p) for p in y_peers]
    z_devices = [device(core, p, x, y) for p in z_peers]

    barrier = pltpu.get_barrier_semaphore()
    friends = [partner] + x_devices[1:] + y_devices[1:] + z_devices[1:]
    friends = friends + halo_friends(lat, lon, lax.axis_size("lat"), lax.axis_size("lon"))
    for friend in friends:
        pl.semaphore_signal(barrier, inc=1, device_id=friend, device_id_type=MESH)

    for which, (left, right) in enumerate(((left_a, right_a), (left_b, right_b))):
        product = lax.dot_general(
            left[...], right[...], (((0,), (0,)), ((), ())), preferred_element_type=jnp.float32
        )
        for block in range(BLOCKS):
            row, col = SIDE * (block // 8), SIDE * (block % 8)
            own[which, block] = product[row : row + SIDE, col : col + SIDE]
    pl.semaphore_wait(barrier, len(friends))

    halo = halo_copies(
        block_ref, edges, halo_low, halo_high, halo_left, halo_right, halo_ssem, halo_rsem
    )
    halo_start(halo, halo_low, halo_high, halo_left, halo_right)
    copies = [
        start_remote(own.at[1 - core], other, core_ssem.at[0], core_rsem.at[0], partner),
        start_remote(dw_ref.at[1 - core], dw_other, core_ssem.at[1], core_rsem.at[1], partner),
    ]
    for copy in copies:
        copy.wait()
    for block in range(BLOCKS):
        bx, by = block // 4, block % 4
        top[bx, by] = own[core, block, :SPLIT] + other[block, :SPLIT]
        low[by, bx, : SIDE - SPLIT] = own[core, block, SPLIT:] + other[block, SPLIT:]
        rows = slice(DW_ROWS * block, DW_ROWS * (block + 1))
        dw_sum = dw_ref[core, rows] + dw_other[rows]
        low[by, bx, SIDE - SPLIT :] = jnp.concatenate(
            [dw_sum, jnp.zeros((DW_PAD - DW_ROWS, SIDE), jnp.float32)], axis=0
        )

    copies = []
    for d in (2, 1, 3):
        copies.append(
            start_remote(top.at[x_peers[d]], top_in1.at[d], xy_ssem.at[0, d], xy_rsem.at[0, d], x_devices[d])
        )
        copies.append(
            start_remote(low.at[y_peers[d]], low_in1.at[d], xy_ssem.at[1, d], xy_rsem.at[1, d], y_devices[d])
        )
    for copy in copies:
        copy.wait()
    top1[...] = top[x] + top_in1[1] + top_in1[2] + top_in1[3]
    low1[...] = low[y] + low_in1[1] + low_in1[2] + low_in1[3]

    copies = []
    for d in (2, 1, 3):
        copies.append(
            start_remote(top1.at[y_peers[d]], top_in2.at[d], xy_ssem.at[2, d], xy_rsem.at[2, d], y_devices[d])
        )
        copies.append(
            start_remote(low1.at[x_peers[d]], low_in2.at[d], xy_ssem.at[3, d], xy_rsem.at[3, d], x_devices[d])
        )
    for copy in copies:
        copy.wait()
    top2 = top1[y] + top_in2[1] + top_in2[2] + top_in2[3]
    low2 = low1[x] + low_in2[1] + low_in2[2] + low_in2[3]
    for tile in range(CHIPS_Z):
        at = TILE * tile
        z_send[tile, :TILE] = top2[at : at + TILE] if at < SPLIT else low2[at - SPLIT : at - SPLIT + TILE]
        z_send[tile, TILE:] = low2[SIDE - SPLIT : SIDE - SPLIT + TILE]

    order = [8, 7, 9, 6, 10, 5, 11, 4, 12, 3, 13, 2, 14, 1, 15]
    copies = []
    for d in order:
        copies.append(
            start_remote(z_send.at[z_peers[d]], z_in.at[z], z_ssem.at[0, d], z_rsem.at[0, d], z_devices[d])
        )
    z_in[z] = z_send[z]
    for copy in copies:
        copy.wait()
    total = z_in[0]
    for tile in range(1, CHIPS_Z):
        total = total + z_in[tile]
    z_own[...] = total

    copies = []
    for d in order:
        copies.append(
            start_remote(z_own.at[:TILE], z_all.at[z], z_ssem.at[1, d], z_rsem.at[1, d], z_devices[d])
        )
    z_all[z] = z_own[:TILE]
    for copy in copies:
        copy.wait()
    tiles = z_all[...].reshape(SIDE, SIDE)
    dw_tile = jnp.concatenate(
        [z_own[TILE:], jnp.zeros((DW_PAD - TILE, SIDE), jnp.float32)], axis=0
    )
    top_g1[y] = tiles[:SPLIT].astype(jnp.bfloat16)
    low_g1[x] = jnp.concatenate([tiles[SPLIT:], dw_tile], axis=0).astype(jnp.bfloat16)

    copies = []
    for d in (2, 1, 3):
        copies.append(
            start_remote(top_g1.at[y], top_g1.at[y], xy_ssem.at[4, d], xy_rsem.at[4, d], y_devices[d])
        )
        copies.append(
            start_remote(low_g1.at[x], low_g1.at[x], xy_ssem.at[5, d], xy_rsem.at[5, d], x_devices[d])
        )
    for copy in copies:
        copy.wait()

    copies = []
    for d in (2, 1, 3):
        copies.append(
            start_remote(top_g1, top_all.at[core, x], xy_ssem.at[6, d], xy_rsem.at[6, d], x_devices[d])
        )
        copies.append(
            start_remote(low_g1, low_all.at[core, y], xy_ssem.at[7, d], xy_rsem.at[7, d], y_devices[d])
        )
    top_all[core, x] = top_g1[...]
    low_all[core, y] = low_g1[...]
    for copy in copies:
        copy.wait()

    copies = [
        start_remote(top_all.at[core], top_all.at[core], core_ssem.at[2], core_rsem.at[2], partner),
        start_remote(low_all.at[core], low_all.at[core], core_ssem.at[3], core_rsem.at[3], partner),
    ]
    for copy in copies:
        copy.wait()
    for which, out in enumerate((out_a, out_b)):
        for block in range(BLOCKS):
            bx, by = block // 4, block % 4
            row, col = SIDE * (block // 8), SIDE * (block % 8)
            out[row : row + SPLIT, col : col + SIDE] = top_all[which, bx, by]
            out[row + SPLIT : row + SIDE, col : col + SIDE] = low_all[which, by, bx, : SIDE - SPLIT]
            dw_rows = low_all[which, by, bx, SIDE - SPLIT :].astype(jnp.float32)[:DW_ROWS]
            out_dw[which, DW_ROWS * block : DW_ROWS * (block + 1)] = dw_rows
    halo_wait(halo)


def sum_gradients(left_a, right_a, left_b, right_b, dw, grid, edges):
    f32, bf16 = jnp.float32, jnp.bfloat16
    vmem = pl.BlockSpec(memory_space=pltpu.VMEM)
    shape = (left_a.shape[1], right_a.shape[1])
    return pl.pallas_call(
        sum_kernel,
        out_shape=(
            jax.ShapeDtypeStruct(shape, bf16),
            jax.ShapeDtypeStruct(shape, bf16),
            jax.ShapeDtypeStruct(dw.shape, f32),
        )
        + halo_shapes(grid),
        in_specs=[vmem] * 7,
        out_specs=(vmem,) * 7,
        scratch_shapes=[
            pltpu.VMEM((2, BLOCKS, SIDE, SIDE), f32),
            pltpu.VMEM((BLOCKS, SIDE, SIDE), f32),
            pltpu.VMEM(dw.shape[1:], f32),
            pltpu.VMEM((4, 4, SPLIT, SIDE), f32),
            pltpu.VMEM((4, 4, LOWER, SIDE), f32),
            pltpu.VMEM((4, 4, SPLIT, SIDE), f32),
            pltpu.VMEM((4, 4, LOWER, SIDE), f32),
            pltpu.VMEM((4, SPLIT, SIDE), f32),
            pltpu.VMEM((4, LOWER, SIDE), f32),
            pltpu.VMEM((4, SPLIT, SIDE), f32),
            pltpu.VMEM((4, LOWER, SIDE), f32),
            pltpu.VMEM((CHIPS_Z, 2 * TILE, SIDE), f32),
            pltpu.VMEM((CHIPS_Z, 2 * TILE, SIDE), f32),
            pltpu.VMEM((2 * TILE, SIDE), f32),
            pltpu.VMEM((CHIPS_Z, TILE, SIDE), f32),
            pltpu.VMEM((4, SPLIT, SIDE), bf16),
            pltpu.VMEM((4, LOWER, SIDE), bf16),
            pltpu.VMEM((2, 4, 4, SPLIT, SIDE), bf16),
            pltpu.VMEM((2, 4, 4, LOWER, SIDE), bf16),
            pltpu.SemaphoreType.DMA((4,)),
            pltpu.SemaphoreType.DMA((4,)),
            pltpu.SemaphoreType.DMA((8, 4)),
            pltpu.SemaphoreType.DMA((8, 4)),
            pltpu.SemaphoreType.DMA((2, CHIPS_Z)),
            pltpu.SemaphoreType.DMA((2, CHIPS_Z)),
            pltpu.SemaphoreType.DMA((8,)),
            pltpu.SemaphoreType.DMA((8,)),
        ],
        compiler_params=pltpu.CompilerParams(collective_id=0, has_side_effects=True),
    )(left_a, right_a, left_b, right_b, dw, grid, edges)


def gelu_tanh(values):
    tanh_arg = slope_coef * (values + cubic_coef * values * values * values)
    return 0.5 * values * (1.0 + jnp.tanh(tanh_arg))


def gelu_slope(values):
    tangent = jnp.tanh(slope_coef * (values + cubic_coef * values * values * values))
    return 0.5 * (1.0 + tangent) + 0.5 * values * (1.0 - tangent * tangent) * slope_coef * (
        1.0 + 3.0 * cubic_coef * values * values
    )


def apply_stencil(padded, dw_weight, tile_rows, tile_cols, flipped):
    kernel_size = dw_weight.shape[0]
    result = jnp.zeros((padded.shape[0], tile_rows, tile_cols, padded.shape[3]), jnp.float32)
    for row_off in range(kernel_size):
        for col_off in range(kernel_size):
            row_start = kernel_size - 1 - row_off if flipped else row_off
            col_start = kernel_size - 1 - col_off if flipped else col_off
            result = (
                result
                + dw_weight[row_off, col_off]
                * padded[:, row_start : row_start + tile_rows, col_start : col_start + tile_cols]
            )
    return result


def local(student, teacher, dw_weight, norm_gain, w_in, w_out, layer_scale):
    batch_size, tile_rows, tile_cols, channel_count = student.shape
    kernel_size = dw_weight.shape[0]
    cell_total = batch_size * tile_rows * lax.axis_size("lat") * tile_cols * lax.axis_size("lon")
    lats = lax.axis_size("lat")
    sent = teacher.reshape(batch_size, lats, -1, teacher.shape[2], channel_count)
    sent = sent.transpose(1, 0, 2, 3, 4).reshape(lats, -1, channel_count)
    *halo, came = front_exchange(student, pack_edges(student), sent)
    padded_bf = join_halo(student, *halo)
    padded = padded_bf.astype(jnp.float32)
    smoothed = apply_stencil(padded, dw_weight, tile_rows, tile_cols, False).reshape(
        -1, channel_count
    )
    average = jnp.mean(smoothed, axis=-1, keepdims=True)
    centred = smoothed - average
    variance = jnp.mean(centred * centred, axis=-1, keepdims=True)
    inv_std = lax.rsqrt(variance + norm_eps)
    unit_norm = centred * inv_std
    normed = (unit_norm * norm_gain).astype(jnp.bfloat16)
    preact = jnp.dot(normed, w_in, preferred_element_type=jnp.float32)
    hidden = gelu_tanh(preact).astype(jnp.bfloat16)
    mlp_out = jnp.dot(hidden, w_out, preferred_element_type=jnp.float32)
    output = student.reshape(-1, channel_count).astype(jnp.float32) + layer_scale * mlp_out
    target = came.reshape(lats, batch_size, tile_rows, tile_cols // lats, channel_count)
    target = target.transpose(1, 2, 0, 3, 4)
    misfit = output - target.reshape(-1, channel_count).astype(jnp.float32)
    out_grad = (layer_scale * misfit).astype(jnp.bfloat16)
    hidden_grad = lax.dot_general(
        out_grad, w_out, (((1,), (1,)), ((), ())), preferred_element_type=jnp.float32
    )
    preact_grad = (hidden_grad * gelu_slope(preact)).astype(jnp.bfloat16)
    normed_grad = lax.dot_general(
        preact_grad, w_in, (((1,), (1,)), ((), ())), preferred_element_type=jnp.float32
    )
    unit_grad = normed_grad * norm_gain
    first_mean = jnp.mean(unit_grad, axis=-1, keepdims=True)
    second_mean = jnp.mean(unit_grad * unit_norm, axis=-1, keepdims=True)
    conv_grad = (inv_std * (unit_grad - first_mean - unit_norm * second_mean)).astype(jnp.bfloat16)
    conv_grid = conv_grad.reshape(student.shape)
    conv_grad_f = conv_grid.astype(jnp.float32)
    kernel_terms = []
    for row_off in range(kernel_size):
        for col_off in range(kernel_size):
            kernel_terms.append(
                jnp.sum(
                    padded[:, row_off : row_off + tile_rows, col_off : col_off + tile_cols]
                    * conv_grad_f,
                    axis=(0, 1, 2),
                )
            )
    taps = kernel_size * kernel_size
    part_dw = jnp.pad(jnp.stack(kernel_terms), ((0, BLOCKS * DW_ROWS - taps), (0, 0)))
    part_dw = part_dw.reshape(BLOCKS * DW_ROWS, 2, SIDE).transpose(1, 0, 2)
    sum_in, sum_out, sum_dw, *halo = sum_gradients(
        normed, preact_grad, out_grad, hidden, part_dw, conv_grid, pack_edges(conv_grid)
    )
    padded_grad = join_halo(conv_grid, *halo).astype(jnp.float32)
    back_conv = apply_stencil(padded_grad, dw_weight, tile_rows, tile_cols, True)
    grad_student = (misfit.reshape(student.shape) + back_conv).astype(jnp.bfloat16)
    sum_dw = sum_dw.transpose(1, 0, 2)[:taps].reshape(kernel_size, kernel_size, channel_count)
    return (
        grad_student,
        sum_in.astype(jnp.float32) / cell_total,
        sum_out.T.astype(jnp.float32) / cell_total,
        sum_dw / cell_total,
    )


def solution(mesh):
    placed = (
        P(None, "lat", "lon", None),
        P(None, None, ("lon", "lat"), None),
        P(),
        P(),
        P(),
        P(),
        P(),
    )
    return jax.shard_map(
        local,
        mesh=mesh,
        in_specs=placed,
        out_specs=(P(None, "lat", "lon", None), P(), P(), P()),
        check_vma=False,
    )
```

```python
import jax
import jax.numpy as jnp
from jax import lax
from jax.experimental import pallas as pl
from jax.experimental.pallas import tpu as pltpu
from jax.sharding import PartitionSpec as P

slope_coef = 0.7978845608028654
cubic_coef = 0.044715
norm_eps = 1e-06
MESH = pl.DeviceIdType.MESH

def start_remote(source, target, ssem, rsem, device_to):
    copy = pltpu.make_async_remote_copy(
        src_ref=source, dst_ref=target, send_sem=ssem, recv_sem=rsem,
        device_id=device_to, device_id_type=MESH,
    )
    copy.start()
    return copy


WIDTH = 3


def halo_friends(lat, lon, lats, lons):
    steps = [(0, 1), (0, -1), (1, 0), (-1, 0)]
    return [
        {"lat": lax.rem(lat + dl + lats, lats), "lon": lax.rem(lon + dn + lons, lons)}
        for dl, dn in steps
    ]


def halo_copies(block, edges, low, high, left, right, ssem, rsem):
    lats, lons = lax.axis_size("lat"), lax.axis_size("lon")
    lat, lon = lax.axis_index("lat"), lax.axis_index("lon")
    rows = block.shape[1]
    up = {"lat": jnp.minimum(lat + 1, lats - 1), "lon": lon}
    down = {"lat": jnp.maximum(lat - 1, 0), "lon": lon}
    first = lat == 0
    last = lat == lats - 1
    inner_up, inner_down = jnp.logical_not(last), jnp.logical_not(first)
    plan = [
        (edges.at[1], left.at[1], {"lat": lat, "lon": lax.rem(lon + 1, lons)}, None, None),
        (edges.at[0], right.at[1], {"lat": lat, "lon": lax.rem(lon + lons - 1, lons)}, None, None),
        (block.at[:, pl.ds(rows - WIDTH, WIDTH)], low, up, inner_up, inner_down),
        (block.at[:, pl.ds(0, WIDTH)], high, down, inner_down, inner_up),
        (left.at[1], left.at[0], up, inner_up, inner_down),
        (right.at[1], right.at[0], up, inner_up, inner_down),
        (left.at[1], left.at[2], down, inner_down, inner_up),
        (right.at[1], right.at[2], down, inner_down, inner_up),
    ]
    copies = []
    for k, (source, target, device_to, sends, comes) in enumerate(plan):
        copy = pltpu.make_async_remote_copy(
            src_ref=source, dst_ref=target, send_sem=ssem.at[k], recv_sem=rsem.at[k],
            device_id=device_to, device_id_type=MESH,
        )
        copies.append((copy, sends, comes))
    return copies


def run_if(condition, action):
    if condition is None:
        action()
    else:
        pl.when(condition)(action)


def halo_start(copies, low, high, left, right):
    lats, lat = lax.axis_size("lat"), lax.axis_index("lat")
    for copy, sends, _ in copies[:4]:
        run_if(sends, copy.start)

    @pl.when(lat == 0)
    def _():
        low[...] = jnp.zeros_like(low)
        left[0] = jnp.zeros(left.shape[1:], left.dtype)
        right[0] = jnp.zeros(right.shape[1:], right.dtype)

    @pl.when(lat == lats - 1)
    def _():
        high[...] = jnp.zeros_like(high)
        left[2] = jnp.zeros(left.shape[1:], left.dtype)
        right[2] = jnp.zeros(right.shape[1:], right.dtype)


def halo_pass_on(copies):
    for copy, _, _ in copies[:2]:
        copy.wait_recv()
    for copy, sends, _ in copies[4:]:
        run_if(sends, copy.start)


def halo_wait(copies):
    for k, (copy, sends, comes) in enumerate(copies):
        run_if(sends, copy.wait_send)
        if k >= 2:
            run_if(comes, copy.wait_recv)


def halo_shapes(block):
    batch, rows, cols, channels = block.shape
    across = jax.ShapeDtypeStruct((batch, WIDTH, cols, channels), block.dtype)
    along = jax.ShapeDtypeStruct((3, batch * rows * WIDTH, channels), block.dtype)
    return (across, across, along, along)


def pack_edges(block):
    batch, rows, cols, channels = block.shape
    sides = jnp.stack([block[:, :, :WIDTH], block[:, :, cols - WIDTH :]])
    return sides.reshape(2, batch * rows * WIDTH, channels)


def join_halo(block, low, high, left, right):
    batch, rows, cols, channels = block.shape

    def columns(side):
        side = side.reshape(3, batch, rows, WIDTH, channels)
        return jnp.concatenate([side[0, :, rows - WIDTH :], side[1], side[2, :, :WIDTH]], axis=1)

    middle = jnp.concatenate([low, block, high], axis=1)
    return jnp.concatenate([columns(left), middle, columns(right)], axis=2)


def front_kernel(
    block, edges, sent, low, high, left, right, came, halo_ssem, halo_rsem, ssem, rsem, local_sem
):
    lats, lons = lax.axis_size("lat"), lax.axis_size("lon")
    lat, lon = lax.axis_index("lat"), lax.axis_index("lon")
    peers = [lax.rem(lat + d, lats) for d in range(lats)]
    friends = halo_friends(lat, lon, lats, lons)[:2] + [{"lat": p, "lon": lon} for p in peers[1:]]
    barrier = pltpu.get_barrier_semaphore()
    for friend in friends:
        pl.semaphore_signal(barrier, inc=1, device_id=friend, device_id_type=MESH)
    mine = pltpu.make_async_copy(sent.at[lat], came.at[lat], local_sem)
    mine.start()
    pl.semaphore_wait(barrier, len(friends))
    halo = halo_copies(block, edges, low, high, left, right, halo_ssem, halo_rsem)
    halo_start(halo, low, high, left, right)
    copies = [
        start_remote(
            sent.at[peers[d]], came.at[lat], ssem.at[d], rsem.at[d], {"lat": peers[d], "lon": lon}
        )
        for d in range(1, lats)
    ]
    halo_pass_on(halo)
    halo_wait(halo)
    mine.wait()
    for copy in copies:
        copy.wait()


def front_exchange(block, edges, sent):
    vmem = pl.BlockSpec(memory_space=pltpu.VMEM)
    lats = sent.shape[0]
    return pl.pallas_call(
        front_kernel,
        out_shape=halo_shapes(block) + (jax.ShapeDtypeStruct(sent.shape, sent.dtype),),
        in_specs=[vmem] * 3,
        out_specs=(vmem,) * 5,
        scratch_shapes=[
            pltpu.SemaphoreType.DMA((8,)),
            pltpu.SemaphoreType.DMA((8,)),
            pltpu.SemaphoreType.DMA((lats,)),
            pltpu.SemaphoreType.DMA((lats,)),
            pltpu.SemaphoreType.DMA,
        ],
        compiler_params=pltpu.CompilerParams(collective_id=1, has_side_effects=True),
    )(block, edges, sent)


BLOCKS, SIDE, SPLIT, TILE, DW_ROWS, DW_PAD = 16, 128, 64, 8, 4, 16
LOWER = SIDE - SPLIT + DW_PAD
CHIPS_Z = 16


def sum_kernel(
    left_a, right_a, left_b, right_b, dw_ref, block_ref, edges,
    out_a, out_b, out_dw, halo_low, halo_high, halo_left, halo_right,
    own, other, dw_other, top, low, top_in1, low_in1, top1, low1, top_in2, low_in2,
    z_send, z_in, z_own, z_all, top_g1, low_g1, top_all, low_all,
    core_ssem, core_rsem, xy_ssem, xy_rsem, z_ssem, z_rsem, halo_ssem, halo_rsem,
):
    lat, lon = lax.axis_index("lat"), lax.axis_index("lon")
    core = lax.rem(lat, 2)
    z = lax.rem(lon, 2) * 8 + lat // 2
    x = lon // 8
    y = lax.rem(lon // 2, 4)

    def device(core_to, z_to, x_to, y_to):
        return {
            "lat": lax.rem(z_to, 8) * 2 + core_to,
            "lon": x_to * 8 + y_to * 2 + z_to // 8,
        }

    partner = device(1 - core, z, x, y)
    x_peers = [lax.rem(x + d, 4) for d in range(4)]
    y_peers = [lax.rem(y + d, 4) for d in range(4)]
    z_peers = [lax.rem(z + d, CHIPS_Z) for d in range(CHIPS_Z)]
    x_devices = [device(core, z, p, y) for p in x_peers]
    y_devices = [device(core, z, x, p) for p in y_peers]
    z_devices = [device(core, p, x, y) for p in z_peers]

    barrier = pltpu.get_barrier_semaphore()
    friends = [partner] + x_devices[1:] + y_devices[1:] + z_devices[1:]
    friends = friends + halo_friends(lat, lon, lax.axis_size("lat"), lax.axis_size("lon"))
    for friend in friends:
        pl.semaphore_signal(barrier, inc=1, device_id=friend, device_id_type=MESH)

    for which, (left, right) in enumerate(((left_a, right_a), (left_b, right_b))):
        product = lax.dot_general(
            left[...], right[...], (((0,), (0,)), ((), ())), preferred_element_type=jnp.float32
        )
        for block in range(BLOCKS):
            row, col = SIDE * (block // 8), SIDE * (block % 8)
            own[which, block] = product[row : row + SIDE, col : col + SIDE]
    pl.semaphore_wait(barrier, len(friends))

    halo = halo_copies(
        block_ref, edges, halo_low, halo_high, halo_left, halo_right, halo_ssem, halo_rsem
    )
    halo_start(halo, halo_low, halo_high, halo_left, halo_right)
    copies = [
        start_remote(own.at[1 - core], other, core_ssem.at[0], core_rsem.at[0], partner),
        start_remote(dw_ref.at[1 - core], dw_other, core_ssem.at[1], core_rsem.at[1], partner),
    ]
    for copy in copies:
        copy.wait()
    for block in range(BLOCKS):
        bx, by = block // 4, block % 4
        top[bx, by] = own[core, block, :SPLIT] + other[block, :SPLIT]
        low[by, bx, : SIDE - SPLIT] = own[core, block, SPLIT:] + other[block, SPLIT:]
        rows = slice(DW_ROWS * block, DW_ROWS * (block + 1))
        dw_sum = dw_ref[core, rows] + dw_other[rows]
        low[by, bx, SIDE - SPLIT :] = jnp.concatenate(
            [dw_sum, jnp.zeros((DW_PAD - DW_ROWS, SIDE), jnp.float32)], axis=0
        )

    copies = []
    for d in (2, 1, 3):
        copies.append(
            start_remote(top.at[x_peers[d]], top_in1.at[d], xy_ssem.at[0, d], xy_rsem.at[0, d], x_devices[d])
        )
        copies.append(
            start_remote(low.at[y_peers[d]], low_in1.at[d], xy_ssem.at[1, d], xy_rsem.at[1, d], y_devices[d])
        )
    for copy in copies:
        copy.wait()
    top1[...] = top[x] + top_in1[1] + top_in1[2] + top_in1[3]
    low1[...] = low[y] + low_in1[1] + low_in1[2] + low_in1[3]

    copies = []
    for d in (2, 1, 3):
        copies.append(
            start_remote(top1.at[y_peers[d]], top_in2.at[d], xy_ssem.at[2, d], xy_rsem.at[2, d], y_devices[d])
        )
        copies.append(
            start_remote(low1.at[x_peers[d]], low_in2.at[d], xy_ssem.at[3, d], xy_rsem.at[3, d], x_devices[d])
        )
    for copy in copies:
        copy.wait()
    top2 = top1[y] + top_in2[1] + top_in2[2] + top_in2[3]
    low2 = low1[x] + low_in2[1] + low_in2[2] + low_in2[3]
    for tile in range(CHIPS_Z):
        at = TILE * tile
        z_send[tile, :TILE] = top2[at : at + TILE] if at < SPLIT else low2[at - SPLIT : at - SPLIT + TILE]
        z_send[tile, TILE:] = low2[SIDE - SPLIT : SIDE - SPLIT + TILE]

    order = [8, 7, 9, 6, 10, 5, 11, 4, 12, 3, 13, 2, 14, 1, 15]
    copies = []
    for d in order:
        copies.append(
            start_remote(z_send.at[z_peers[d]], z_in.at[z], z_ssem.at[0, d], z_rsem.at[0, d], z_devices[d])
        )
    z_in[z] = z_send[z]
    halo_pass_on(halo)
    for copy in copies:
        copy.wait()
    total = z_in[0]
    for tile in range(1, CHIPS_Z):
        total = total + z_in[tile]
    z_own[...] = total

    copies = []
    for d in order:
        copies.append(
            start_remote(z_own.at[:TILE], z_all.at[z], z_ssem.at[1, d], z_rsem.at[1, d], z_devices[d])
        )
    z_all[z] = z_own[:TILE]
    for copy in copies:
        copy.wait()
    tiles = z_all[...].reshape(SIDE, SIDE)
    dw_tile = jnp.concatenate(
        [z_own[TILE:], jnp.zeros((DW_PAD - TILE, SIDE), jnp.float32)], axis=0
    )
    top_g1[y] = tiles[:SPLIT].astype(jnp.bfloat16)
    low_g1[x] = jnp.concatenate([tiles[SPLIT:], dw_tile], axis=0).astype(jnp.bfloat16)

    copies = []
    for d in (2, 1, 3):
        copies.append(
            start_remote(top_g1.at[y], top_g1.at[y], xy_ssem.at[4, d], xy_rsem.at[4, d], y_devices[d])
        )
        copies.append(
            start_remote(low_g1.at[x], low_g1.at[x], xy_ssem.at[5, d], xy_rsem.at[5, d], x_devices[d])
        )
    for copy in copies:
        copy.wait()

    copies = []
    for d in (2, 1, 3):
        copies.append(
            start_remote(top_g1, top_all.at[core, x], xy_ssem.at[6, d], xy_rsem.at[6, d], x_devices[d])
        )
        copies.append(
            start_remote(low_g1, low_all.at[core, y], xy_ssem.at[7, d], xy_rsem.at[7, d], y_devices[d])
        )
    top_all[core, x] = top_g1[...]
    low_all[core, y] = low_g1[...]
    for copy in copies:
        copy.wait()

    copies = [
        start_remote(top_all.at[core], top_all.at[core], core_ssem.at[2], core_rsem.at[2], partner),
        start_remote(low_all.at[core], low_all.at[core], core_ssem.at[3], core_rsem.at[3], partner),
    ]
    for copy in copies:
        copy.wait()
    for which, out in enumerate((out_a, out_b)):
        for block in range(BLOCKS):
            bx, by = block // 4, block % 4
            row, col = SIDE * (block // 8), SIDE * (block % 8)
            out[row : row + SPLIT, col : col + SIDE] = top_all[which, bx, by]
            out[row + SPLIT : row + SIDE, col : col + SIDE] = low_all[which, by, bx, : SIDE - SPLIT]
            dw_rows = low_all[which, by, bx, SIDE - SPLIT :].astype(jnp.float32)[:DW_ROWS]
            out_dw[which, DW_ROWS * block : DW_ROWS * (block + 1)] = dw_rows
    halo_wait(halo)


def sum_gradients(left_a, right_a, left_b, right_b, dw, grid, edges):
    f32, bf16 = jnp.float32, jnp.bfloat16
    vmem = pl.BlockSpec(memory_space=pltpu.VMEM)
    shape = (left_a.shape[1], right_a.shape[1])
    return pl.pallas_call(
        sum_kernel,
        out_shape=(
            jax.ShapeDtypeStruct(shape, bf16),
            jax.ShapeDtypeStruct(shape, bf16),
            jax.ShapeDtypeStruct(dw.shape, f32),
        )
        + halo_shapes(grid),
        in_specs=[vmem] * 7,
        out_specs=(vmem,) * 7,
        scratch_shapes=[
            pltpu.VMEM((2, BLOCKS, SIDE, SIDE), f32),
            pltpu.VMEM((BLOCKS, SIDE, SIDE), f32),
            pltpu.VMEM(dw.shape[1:], f32),
            pltpu.VMEM((4, 4, SPLIT, SIDE), f32),
            pltpu.VMEM((4, 4, LOWER, SIDE), f32),
            pltpu.VMEM((4, 4, SPLIT, SIDE), f32),
            pltpu.VMEM((4, 4, LOWER, SIDE), f32),
            pltpu.VMEM((4, SPLIT, SIDE), f32),
            pltpu.VMEM((4, LOWER, SIDE), f32),
            pltpu.VMEM((4, SPLIT, SIDE), f32),
            pltpu.VMEM((4, LOWER, SIDE), f32),
            pltpu.VMEM((CHIPS_Z, 2 * TILE, SIDE), f32),
            pltpu.VMEM((CHIPS_Z, 2 * TILE, SIDE), f32),
            pltpu.VMEM((2 * TILE, SIDE), f32),
            pltpu.VMEM((CHIPS_Z, TILE, SIDE), f32),
            pltpu.VMEM((4, SPLIT, SIDE), bf16),
            pltpu.VMEM((4, LOWER, SIDE), bf16),
            pltpu.VMEM((2, 4, 4, SPLIT, SIDE), bf16),
            pltpu.VMEM((2, 4, 4, LOWER, SIDE), bf16),
            pltpu.SemaphoreType.DMA((4,)),
            pltpu.SemaphoreType.DMA((4,)),
            pltpu.SemaphoreType.DMA((8, 4)),
            pltpu.SemaphoreType.DMA((8, 4)),
            pltpu.SemaphoreType.DMA((2, CHIPS_Z)),
            pltpu.SemaphoreType.DMA((2, CHIPS_Z)),
            pltpu.SemaphoreType.DMA((8,)),
            pltpu.SemaphoreType.DMA((8,)),
        ],
        compiler_params=pltpu.CompilerParams(collective_id=0, has_side_effects=True),
    )(left_a, right_a, left_b, right_b, dw, grid, edges)


def gelu_tanh(values):
    tanh_arg = slope_coef * (values + cubic_coef * values * values * values)
    return 0.5 * values * (1.0 + jnp.tanh(tanh_arg))


def gelu_slope(values):
    tangent = jnp.tanh(slope_coef * (values + cubic_coef * values * values * values))
    return 0.5 * (1.0 + tangent) + 0.5 * values * (1.0 - tangent * tangent) * slope_coef * (
        1.0 + 3.0 * cubic_coef * values * values
    )


def apply_stencil(padded, dw_weight, tile_rows, tile_cols, flipped):
    kernel_size = dw_weight.shape[0]
    result = jnp.zeros((padded.shape[0], tile_rows, tile_cols, padded.shape[3]), jnp.float32)
    for row_off in range(kernel_size):
        for col_off in range(kernel_size):
            row_start = kernel_size - 1 - row_off if flipped else row_off
            col_start = kernel_size - 1 - col_off if flipped else col_off
            result = (
                result
                + dw_weight[row_off, col_off]
                * padded[:, row_start : row_start + tile_rows, col_start : col_start + tile_cols]
            )
    return result


def local(student, teacher, dw_weight, norm_gain, w_in, w_out, layer_scale):
    batch_size, tile_rows, tile_cols, channel_count = student.shape
    kernel_size = dw_weight.shape[0]
    cell_total = batch_size * tile_rows * lax.axis_size("lat") * tile_cols * lax.axis_size("lon")
    lats = lax.axis_size("lat")
    sent = teacher.reshape(batch_size, lats, -1, teacher.shape[2], channel_count)
    sent = sent.transpose(1, 0, 2, 3, 4).reshape(lats, -1, channel_count)
    *halo, came = front_exchange(student, pack_edges(student), sent)
    padded_bf = join_halo(student, *halo)
    padded = padded_bf.astype(jnp.float32)
    smoothed = apply_stencil(padded, dw_weight, tile_rows, tile_cols, False).reshape(
        -1, channel_count
    )
    average = jnp.mean(smoothed, axis=-1, keepdims=True)
    centred = smoothed - average
    variance = jnp.mean(centred * centred, axis=-1, keepdims=True)
    inv_std = lax.rsqrt(variance + norm_eps)
    unit_norm = centred * inv_std
    normed = (unit_norm * norm_gain).astype(jnp.bfloat16)
    preact = jnp.dot(normed, w_in, preferred_element_type=jnp.float32)
    hidden = gelu_tanh(preact).astype(jnp.bfloat16)
    mlp_out = jnp.dot(hidden, w_out, preferred_element_type=jnp.float32)
    output = student.reshape(-1, channel_count).astype(jnp.float32) + layer_scale * mlp_out
    target = came.reshape(lats, batch_size, tile_rows, tile_cols // lats, channel_count)
    target = target.transpose(1, 2, 0, 3, 4)
    misfit = output - target.reshape(-1, channel_count).astype(jnp.float32)
    out_grad = (layer_scale * misfit).astype(jnp.bfloat16)
    hidden_grad = lax.dot_general(
        out_grad, w_out, (((1,), (1,)), ((), ())), preferred_element_type=jnp.float32
    )
    preact_grad = (hidden_grad * gelu_slope(preact)).astype(jnp.bfloat16)
    normed_grad = lax.dot_general(
        preact_grad, w_in, (((1,), (1,)), ((), ())), preferred_element_type=jnp.float32
    )
    unit_grad = normed_grad * norm_gain
    first_mean = jnp.mean(unit_grad, axis=-1, keepdims=True)
    second_mean = jnp.mean(unit_grad * unit_norm, axis=-1, keepdims=True)
    conv_grad = (inv_std * (unit_grad - first_mean - unit_norm * second_mean)).astype(jnp.bfloat16)
    conv_grid = conv_grad.reshape(student.shape)
    conv_grad_f = conv_grid.astype(jnp.float32)
    kernel_terms = []
    for row_off in range(kernel_size):
        for col_off in range(kernel_size):
            kernel_terms.append(
                jnp.sum(
                    padded[:, row_off : row_off + tile_rows, col_off : col_off + tile_cols]
                    * conv_grad_f,
                    axis=(0, 1, 2),
                )
            )
    taps = kernel_size * kernel_size
    part_dw = jnp.pad(jnp.stack(kernel_terms), ((0, BLOCKS * DW_ROWS - taps), (0, 0)))
    part_dw = part_dw.reshape(BLOCKS * DW_ROWS, 2, SIDE).transpose(1, 0, 2)
    sum_in, sum_out, sum_dw, *halo = sum_gradients(
        normed, preact_grad, out_grad, hidden, part_dw, conv_grid, pack_edges(conv_grid)
    )
    padded_grad = join_halo(conv_grid, *halo).astype(jnp.float32)
    back_conv = apply_stencil(padded_grad, dw_weight, tile_rows, tile_cols, True)
    grad_student = (misfit.reshape(student.shape) + back_conv).astype(jnp.bfloat16)
    sum_dw = sum_dw.transpose(1, 0, 2)[:taps].reshape(kernel_size, kernel_size, channel_count)
    return (
        grad_student,
        sum_in.astype(jnp.float32) / cell_total,
        sum_out.T.astype(jnp.float32) / cell_total,
        sum_dw / cell_total,
    )


def solution(mesh):
    placed = (
        P(None, "lat", "lon", None),
        P(None, None, ("lon", "lat"), None),
        P(),
        P(),
        P(),
        P(),
        P(),
    )
    return jax.shard_map(
        local,
        mesh=mesh,
        in_specs=placed,
        out_specs=(P(None, "lat", "lon", None), P(), P(), P()),
        check_vma=False,
    )
```

```python
import jax
import jax.numpy as jnp
from jax import lax
from jax.experimental import pallas as pl
from jax.experimental.pallas import tpu as pltpu
from jax.sharding import PartitionSpec as P

slope_coef = 0.7978845608028654
cubic_coef = 0.044715
norm_eps = 1e-06
MESH = pl.DeviceIdType.MESH

def start_remote(source, target, ssem, rsem, device_to):
    copy = pltpu.make_async_remote_copy(
        src_ref=source, dst_ref=target, send_sem=ssem, recv_sem=rsem,
        device_id=device_to, device_id_type=MESH,
    )
    copy.start()
    return copy


WIDTH = 3


def halo_friends(lat, lon, lats, lons):
    steps = [(0, 1), (0, -1), (1, 0), (-1, 0)]
    return [
        {"lat": lax.rem(lat + dl + lats, lats), "lon": lax.rem(lon + dn + lons, lons)}
        for dl, dn in steps
    ]


def halo_copies(block, edges, low, high, left, right, ssem, rsem):
    lats, lons = lax.axis_size("lat"), lax.axis_size("lon")
    lat, lon = lax.axis_index("lat"), lax.axis_index("lon")
    rows = block.shape[1]
    up = {"lat": jnp.minimum(lat + 1, lats - 1), "lon": lon}
    down = {"lat": jnp.maximum(lat - 1, 0), "lon": lon}
    first = lat == 0
    last = lat == lats - 1
    inner_up, inner_down = jnp.logical_not(last), jnp.logical_not(first)
    plan = [
        (edges.at[1], left.at[1], {"lat": lat, "lon": lax.rem(lon + 1, lons)}, None, None),
        (edges.at[0], right.at[1], {"lat": lat, "lon": lax.rem(lon + lons - 1, lons)}, None, None),
        (block.at[:, pl.ds(rows - WIDTH, WIDTH)], low, up, inner_up, inner_down),
        (block.at[:, pl.ds(0, WIDTH)], high, down, inner_down, inner_up),
        (left.at[1], left.at[0], up, inner_up, inner_down),
        (right.at[1], right.at[0], up, inner_up, inner_down),
        (left.at[1], left.at[2], down, inner_down, inner_up),
        (right.at[1], right.at[2], down, inner_down, inner_up),
    ]
    copies = []
    for k, (source, target, device_to, sends, comes) in enumerate(plan):
        copy = pltpu.make_async_remote_copy(
            src_ref=source, dst_ref=target, send_sem=ssem.at[k], recv_sem=rsem.at[k],
            device_id=device_to, device_id_type=MESH,
        )
        copies.append((copy, sends, comes))
    return copies


def run_if(condition, action):
    if condition is None:
        action()
    else:
        pl.when(condition)(action)


def halo_start(copies, low, high, left, right):
    lats, lat = lax.axis_size("lat"), lax.axis_index("lat")
    for copy, sends, _ in copies[:4]:
        run_if(sends, copy.start)

    @pl.when(lat == 0)
    def _():
        low[...] = jnp.zeros_like(low)
        left[0] = jnp.zeros(left.shape[1:], left.dtype)
        right[0] = jnp.zeros(right.shape[1:], right.dtype)

    @pl.when(lat == lats - 1)
    def _():
        high[...] = jnp.zeros_like(high)
        left[2] = jnp.zeros(left.shape[1:], left.dtype)
        right[2] = jnp.zeros(right.shape[1:], right.dtype)


def halo_pass_on(copies):
    for copy, _, _ in copies[:2]:
        copy.wait_recv()
    for copy, sends, _ in copies[4:]:
        run_if(sends, copy.start)


def halo_wait(copies):
    for k, (copy, sends, comes) in enumerate(copies):
        run_if(sends, copy.wait_send)
        if k >= 2:
            run_if(comes, copy.wait_recv)


def pack_edges(block, rows_f32, edges):
    batch, rows, cols, channels = block.shape
    for b in range(batch):
        for row in range(rows):
            at = (b * rows + row) * WIDTH
            line = block[b, row].astype(jnp.float32)
            rows_f32[0, at : at + WIDTH] = line[:WIDTH]
            rows_f32[1, at : at + WIDTH] = line[cols - WIDTH :]
    edges[...] = rows_f32[...].astype(edges.dtype)


def fill_padded(padded, edge_rows, block, low, high, left, right):
    batch, rows, cols, channels = block.shape
    for side, ref in enumerate((left, right)):
        for k in range(3):
            edge_rows[side, k] = ref[k].astype(jnp.float32)
    for b in range(batch):
        for row in range(rows + 2 * WIDTH):
            if row < WIDTH:
                line, k, r = low[b, row], 0, rows - WIDTH + row
            elif row < WIDTH + rows:
                line, k, r = block[b, row - WIDTH], 1, row - WIDTH
            else:
                line, k, r = high[b, row - WIDTH - rows], 2, row - WIDTH - rows
            at = (b * rows + r) * WIDTH
            padded[b, row, WIDTH : WIDTH + cols] = line.astype(jnp.float32)
            padded[b, row, :WIDTH] = edge_rows[0, k, at : at + WIDTH]
            padded[b, row, WIDTH + cols : 2 * WIDTH + cols] = edge_rows[1, k, at : at + WIDTH]


def run_stencil(padded, weight, shape, flipped, emit):
    batch, rows, cols, channels = shape
    size = weight.shape[0]

    @pl.loop(0, batch * rows)
    def _(n):
        b, row = n // rows, lax.rem(n, rows)
        total = jnp.zeros((cols, channels), jnp.float32)
        for p in range(size):
            for q in range(size):
                row_at = size - 1 - p if flipped else p
                col_at = size - 1 - q if flipped else q
                total = total + weight[p, q : q + 1] * padded[b, row + row_at, col_at : col_at + cols]
        emit(n, b, row, total)


def tap_sums(padded, cell_grad, shape, size, dw):
    batch, rows, cols, channels = shape
    dw[...] = jnp.zeros_like(dw)

    @pl.loop(0, size)
    def _(p):
        for q in range(size):
            total = jnp.zeros((TILE, channels), jnp.float32)
            for n in range(batch * rows):
                b, row = n // rows, n % rows
                product = padded[b, row + p, q : q + cols] * cell_grad[n * cols : (n + 1) * cols]
                for t in range(cols // TILE):
                    total = total + product[t * TILE : (t + 1) * TILE]
            line = jnp.sum(total, axis=0, keepdims=True)
            for half in range(2):
                dw[half, pl.ds(p * TILE + q, 1)] = line[:, half * SIDE : (half + 1) * SIDE]


BLOCKS, SIDE, SPLIT, TILE, DW_ROWS, DW_PAD = 16, 128, 64, 8, 4, 16
LOWER = SIDE - SPLIT + DW_PAD
CHIPS_Z = 16
CHUNK = 256


def step_kernel(
    block, sent, weight, gain, w_in, w_out, scale,
    out_a, out_b, out_dw, out_grad_ref,
    edge_f32, edges, low, high, left, right, edge_rows, padded, came, came_f32, target,
    smoothed, unit, hid, slope, misfit, cell_grad, grad_block,
    edges2, low2h, high2h, left2h, right2h, padded2, dw_ref,
    own, other, dw_other, top, low_part, top_in1, low_in1, top1, low1, top_in2, low_in2,
    z_send, z_in, z_own, z_all, top_g1, low_g1, top_all, low_all,
    core_ssem, core_rsem, xy_ssem, xy_rsem, z_ssem, z_rsem, halo_ssem, halo_rsem,
    halo2_ssem, halo2_rsem, teach_ssem, teach_rsem, local_sem,
):
    f32, bf16 = jnp.float32, jnp.bfloat16
    lats, lons = lax.axis_size("lat"), lax.axis_size("lon")
    lat, lon = lax.axis_index("lat"), lax.axis_index("lon")
    core = lax.rem(lat, 2)
    z = lax.rem(lon, 2) * 8 + lat // 2
    x = lon // 8
    y = lax.rem(lon // 2, 4)

    def device(core_to, z_to, x_to, y_to):
        return {
            "lat": lax.rem(z_to, 8) * 2 + core_to,
            "lon": x_to * 8 + y_to * 2 + z_to // 8,
        }

    partner = device(1 - core, z, x, y)
    x_peers = [lax.rem(x + d, 4) for d in range(4)]
    y_peers = [lax.rem(y + d, 4) for d in range(4)]
    z_peers = [lax.rem(z + d, CHIPS_Z) for d in range(CHIPS_Z)]
    x_devices = [device(core, z, p, y) for p in x_peers]
    y_devices = [device(core, z, x, p) for p in y_peers]
    z_devices = [device(core, p, x, y) for p in z_peers]

    barrier = pltpu.get_barrier_semaphore()
    friends = [partner] + x_devices[1:] + y_devices[1:] + z_devices[1:]
    lat_peers = [lax.rem(lat + d, lats) for d in range(lats)]
    friends = friends + halo_friends(lat, lon, lats, lons)[:2]
    friends = friends + [{"lat": p, "lon": lon} for p in lat_peers[1:]]
    for friend in friends:
        pl.semaphore_signal(barrier, inc=1, device_id=friend, device_id_type=MESH)

    mine = pltpu.make_async_copy(sent.at[lat], came.at[lat], local_sem)
    mine.start()
    pack_edges(block, edge_f32, edges)
    pl.semaphore_wait(barrier, len(friends))

    front = halo_copies(block, edges, low, high, left, right, halo_ssem, halo_rsem)
    halo_start(front, low, high, left, right)
    teaching = [
        start_remote(
            sent.at[lat_peers[d]], came.at[lat], teach_ssem.at[d], teach_rsem.at[d],
            {"lat": lat_peers[d], "lon": lon},
        )
        for d in range(1, lats)
    ]
    halo_pass_on(front)
    halo_wait(front)
    fill_padded(padded, edge_rows, block, low, high, left, right)

    shape = block.shape
    batch, rows, cols, channels = shape

    def keep(n, b, row, total):
        smoothed[pl.ds(pl.multiple_of(n * cols, cols), cols)] = total

    run_stencil(padded, weight, shape, False, keep)
    smooth = smoothed[...]
    average = jnp.mean(smooth, axis=-1, keepdims=True)
    centred = smooth - average
    variance = jnp.mean(centred * centred, axis=-1, keepdims=True)
    inv_std = lax.rsqrt(variance + norm_eps)
    unit[...] = centred * inv_std
    normed = (unit[...] * gain[...]).astype(bf16)
    mlp_out = jnp.zeros((batch * rows * cols, channels), f32)
    hidden_size = w_in.shape[1]
    for at in range(0, hidden_size, CHUNK):
        preact = jnp.dot(normed, w_in[:, at : at + CHUNK], preferred_element_type=f32)
        tangent = jnp.tanh(slope_coef * (preact + cubic_coef * preact * preact * preact))
        hidden = (0.5 * preact * (1.0 + tangent)).astype(bf16)
        hid[:, at : at + CHUNK] = hidden
        slope[:, at : at + CHUNK] = 0.5 * (1.0 + tangent) + 0.5 * preact * (
            1.0 - tangent * tangent
        ) * slope_coef * (1.0 + 3.0 * cubic_coef * preact * preact)
        mlp_out = mlp_out + jnp.dot(hidden, w_out[at : at + CHUNK], preferred_element_type=f32)

    mine.wait()
    for copy in teaching:
        copy.wait()
    for src in range(lats):
        came_f32[src] = came[src].astype(f32)
    part = cols // lats
    for src in range(lats):
        for n in range(batch * rows):
            at = n * cols + src * part
            target[at : at + part] = came_f32[src, n * part : (n + 1) * part]
    student = jnp.concatenate(
        [block[n // rows, n % rows] for n in range(batch * rows)], axis=0
    ).astype(f32)
    misfit[...] = (student + scale[...] * mlp_out) - target[...]
    out_grad = (scale[...] * misfit[...]).astype(bf16)
    contract_cells = (((0,), (0,)), ((), ()))
    contract_last = (((1,), (1,)), ((), ()))

    def keep_product(which, at, product):
        for row in range(channels // SIDE):
            for col in range(CHUNK // SIDE):
                own[which, row * 8 + at // SIDE + col] = product[
                    row * SIDE : (row + 1) * SIDE, col * SIDE : (col + 1) * SIDE
                ]

    normed_grad = jnp.zeros((batch * rows * cols, channels), f32)
    for at in range(0, hidden_size, CHUNK):
        hidden_grad = lax.dot_general(
            out_grad, w_out[at : at + CHUNK], contract_last, preferred_element_type=f32
        )
        preact_grad = (hidden_grad * slope[:, at : at + CHUNK]).astype(bf16)
        keep_product(
            0, at, lax.dot_general(normed, preact_grad, contract_cells, preferred_element_type=f32)
        )
        keep_product(
            1,
            at,
            lax.dot_general(
                out_grad, hid[:, at : at + CHUNK], contract_cells, preferred_element_type=f32
            ),
        )
        normed_grad = normed_grad + lax.dot_general(
            preact_grad, w_in[:, at : at + CHUNK], contract_last, preferred_element_type=f32
        )
    core_copies = [
        start_remote(own.at[1 - core], other, core_ssem.at[0], core_rsem.at[0], partner)
    ]
    unit_grad = normed_grad * gain[...]
    unit_norm = unit[...]
    first_mean = jnp.mean(unit_grad, axis=-1, keepdims=True)
    second_mean = jnp.mean(unit_grad * unit_norm, axis=-1, keepdims=True)
    conv_grad = (inv_std * (unit_grad - first_mean - unit_norm * second_mean)).astype(bf16)
    for n in range(batch * rows):
        grad_block[n // rows, n % rows] = conv_grad[n * cols : (n + 1) * cols]
    cell_grad[...] = conv_grad.astype(f32)
    pack_edges(grad_block, edge_f32, edges2)
    halo = halo_copies(
        grad_block, edges2, low2h, high2h, left2h, right2h, halo2_ssem, halo2_rsem
    )
    halo_start(halo, low2h, high2h, left2h, right2h)
    tap_sums(padded, cell_grad, shape, weight.shape[0], dw_ref)
    copies = core_copies + [
        start_remote(dw_ref.at[1 - core], dw_other, core_ssem.at[1], core_rsem.at[1], partner),
    ]
    for copy in copies:
        copy.wait()
    for block in range(BLOCKS):
        bx, by = block // 4, block % 4
        top[bx, by] = own[core, block, :SPLIT] + other[block, :SPLIT]
        low_part[by, bx, : SIDE - SPLIT] = own[core, block, SPLIT:] + other[block, SPLIT:]
        rows = slice(DW_ROWS * block, DW_ROWS * (block + 1))
        dw_sum = dw_ref[core, rows] + dw_other[rows]
        low_part[by, bx, SIDE - SPLIT :] = jnp.concatenate(
            [dw_sum, jnp.zeros((DW_PAD - DW_ROWS, SIDE), jnp.float32)], axis=0
        )

    copies = []
    for d in (2, 1, 3):
        copies.append(
            start_remote(top.at[x_peers[d]], top_in1.at[d], xy_ssem.at[0, d], xy_rsem.at[0, d], x_devices[d])
        )
        copies.append(
            start_remote(low_part.at[y_peers[d]], low_in1.at[d], xy_ssem.at[1, d], xy_rsem.at[1, d], y_devices[d])
        )
    for copy in copies:
        copy.wait()
    top1[...] = top[x] + top_in1[1] + top_in1[2] + top_in1[3]
    low1[...] = low_part[y] + low_in1[1] + low_in1[2] + low_in1[3]

    copies = []
    for d in (2, 1, 3):
        copies.append(
            start_remote(top1.at[y_peers[d]], top_in2.at[d], xy_ssem.at[2, d], xy_rsem.at[2, d], y_devices[d])
        )
        copies.append(
            start_remote(low1.at[x_peers[d]], low_in2.at[d], xy_ssem.at[3, d], xy_rsem.at[3, d], x_devices[d])
        )
    for copy in copies:
        copy.wait()
    top2 = top1[y] + top_in2[1] + top_in2[2] + top_in2[3]
    low2 = low1[x] + low_in2[1] + low_in2[2] + low_in2[3]
    for tile in range(CHIPS_Z):
        at = TILE * tile
        z_send[tile, :TILE] = top2[at : at + TILE] if at < SPLIT else low2[at - SPLIT : at - SPLIT + TILE]
        z_send[tile, TILE:] = low2[SIDE - SPLIT : SIDE - SPLIT + TILE]

    order = [8, 7, 9, 6, 10, 5, 11, 4, 12, 3, 13, 2, 14, 1, 15]
    copies = []
    for d in order:
        copies.append(
            start_remote(z_send.at[z_peers[d]], z_in.at[z], z_ssem.at[0, d], z_rsem.at[0, d], z_devices[d])
        )
    z_in[z] = z_send[z]
    halo_pass_on(halo)
    for copy in copies:
        copy.wait()
    total = z_in[0]
    for tile in range(1, CHIPS_Z):
        total = total + z_in[tile]
    z_own[...] = total

    copies = []
    for d in order:
        copies.append(
            start_remote(z_own.at[:TILE], z_all.at[z], z_ssem.at[1, d], z_rsem.at[1, d], z_devices[d])
        )
    z_all[z] = z_own[:TILE]
    for copy in copies:
        copy.wait()
    tiles = z_all[...].reshape(SIDE, SIDE)
    dw_tile = jnp.concatenate(
        [z_own[TILE:], jnp.zeros((DW_PAD - TILE, SIDE), jnp.float32)], axis=0
    )
    top_g1[y] = tiles[:SPLIT].astype(jnp.bfloat16)
    low_g1[x] = jnp.concatenate([tiles[SPLIT:], dw_tile], axis=0).astype(jnp.bfloat16)

    copies = []
    for d in (2, 1, 3):
        copies.append(
            start_remote(top_g1.at[y], top_g1.at[y], xy_ssem.at[4, d], xy_rsem.at[4, d], y_devices[d])
        )
        copies.append(
            start_remote(low_g1.at[x], low_g1.at[x], xy_ssem.at[5, d], xy_rsem.at[5, d], x_devices[d])
        )
    for copy in copies:
        copy.wait()

    copies = []
    for d in (2, 1, 3):
        copies.append(
            start_remote(top_g1, top_all.at[core, x], xy_ssem.at[6, d], xy_rsem.at[6, d], x_devices[d])
        )
        copies.append(
            start_remote(low_g1, low_all.at[core, y], xy_ssem.at[7, d], xy_rsem.at[7, d], y_devices[d])
        )
    top_all[core, x] = top_g1[...]
    low_all[core, y] = low_g1[...]
    halo_wait(halo)
    fill_padded(padded2, edge_rows, grad_block, low2h, high2h, left2h, right2h)

    def finish(n, b, row, total):
        cells = pl.ds(pl.multiple_of(n * cols, cols), cols)
        out_grad_ref[b, row] = (misfit[cells] + total).astype(bf16)

    run_stencil(padded2, weight, shape, True, finish)
    for copy in copies:
        copy.wait()

    copies = [
        start_remote(top_all.at[core], top_all.at[core], core_ssem.at[2], core_rsem.at[2], partner),
        start_remote(low_all.at[core], low_all.at[core], core_ssem.at[3], core_rsem.at[3], partner),
    ]
    for copy in copies:
        copy.wait()
    for which, out in enumerate((out_a, out_b)):
        for block in range(BLOCKS):
            bx, by = block // 4, block % 4
            row, col = SIDE * (block // 8), SIDE * (block % 8)
            out[row : row + SPLIT, col : col + SIDE] = top_all[which, bx, by]
            out[row + SPLIT : row + SIDE, col : col + SIDE] = low_all[which, by, bx, : SIDE - SPLIT]
            dw_rows = low_all[which, by, bx, SIDE - SPLIT :].astype(jnp.float32)[:DW_ROWS]
            out_dw[which, DW_ROWS * block : DW_ROWS * (block + 1)] = dw_rows


def whole_step(block, sent, weight, gain, w_in, w_out, scale):
    f32, bf16 = jnp.float32, jnp.bfloat16
    batch, rows, cols, channels = block.shape
    cells, lats = batch * rows * cols, sent.shape[0]
    edge_cells = batch * rows * WIDTH
    vmem = pl.BlockSpec(memory_space=pltpu.VMEM)
    across = pltpu.VMEM((batch, WIDTH, cols, channels), bf16)
    along = pltpu.VMEM((3, edge_cells, channels), bf16)
    padded = pltpu.VMEM((batch, rows + 2 * WIDTH, cols + 2 * WIDTH + 2, channels), f32)
    dw_shape = (2, BLOCKS * DW_ROWS, SIDE)
    cell_f32 = pltpu.VMEM((cells, channels), f32)
    return pl.pallas_call(
        step_kernel,
        out_shape=(
            jax.ShapeDtypeStruct(w_in.shape, bf16),
            jax.ShapeDtypeStruct(w_in.shape, bf16),
            jax.ShapeDtypeStruct(dw_shape, f32),
            jax.ShapeDtypeStruct(block.shape, bf16),
        ),
        in_specs=[vmem] * 7,
        out_specs=(vmem,) * 4,
        scratch_shapes=[
            pltpu.VMEM((2, edge_cells, channels), f32),
            pltpu.VMEM((2, edge_cells, channels), bf16),
            across,
            across,
            along,
            along,
            pltpu.VMEM((2, 3, edge_cells, channels), f32),
            padded,
            pltpu.VMEM(sent.shape, bf16),
            pltpu.VMEM(sent.shape, f32),
            cell_f32,
            cell_f32,
            cell_f32,
            pltpu.VMEM((cells, w_in.shape[1]), bf16),
            pltpu.VMEM((cells, w_in.shape[1]), f32),
            cell_f32,
            cell_f32,
            pltpu.VMEM(block.shape, bf16),
            pltpu.VMEM((2, edge_cells, channels), bf16),
            across,
            across,
            along,
            along,
            padded,
            pltpu.VMEM(dw_shape, f32),
            pltpu.VMEM((2, BLOCKS, SIDE, SIDE), f32),
            pltpu.VMEM((BLOCKS, SIDE, SIDE), f32),
            pltpu.VMEM(dw_shape[1:], f32),
            pltpu.VMEM((4, 4, SPLIT, SIDE), f32),
            pltpu.VMEM((4, 4, LOWER, SIDE), f32),
            pltpu.VMEM((4, 4, SPLIT, SIDE), f32),
            pltpu.VMEM((4, 4, LOWER, SIDE), f32),
            pltpu.VMEM((4, SPLIT, SIDE), f32),
            pltpu.VMEM((4, LOWER, SIDE), f32),
            pltpu.VMEM((4, SPLIT, SIDE), f32),
            pltpu.VMEM((4, LOWER, SIDE), f32),
            pltpu.VMEM((CHIPS_Z, 2 * TILE, SIDE), f32),
            pltpu.VMEM((CHIPS_Z, 2 * TILE, SIDE), f32),
            pltpu.VMEM((2 * TILE, SIDE), f32),
            pltpu.VMEM((CHIPS_Z, TILE, SIDE), f32),
            pltpu.VMEM((4, SPLIT, SIDE), bf16),
            pltpu.VMEM((4, LOWER, SIDE), bf16),
            pltpu.VMEM((2, 4, 4, SPLIT, SIDE), bf16),
            pltpu.VMEM((2, 4, 4, LOWER, SIDE), bf16),
            pltpu.SemaphoreType.DMA((4,)),
            pltpu.SemaphoreType.DMA((4,)),
            pltpu.SemaphoreType.DMA((8, 4)),
            pltpu.SemaphoreType.DMA((8, 4)),
            pltpu.SemaphoreType.DMA((2, CHIPS_Z)),
            pltpu.SemaphoreType.DMA((2, CHIPS_Z)),
            pltpu.SemaphoreType.DMA((8,)),
            pltpu.SemaphoreType.DMA((8,)),
            pltpu.SemaphoreType.DMA((8,)),
            pltpu.SemaphoreType.DMA((8,)),
            pltpu.SemaphoreType.DMA((lats,)),
            pltpu.SemaphoreType.DMA((lats,)),
            pltpu.SemaphoreType.DMA,
        ],
        compiler_params=pltpu.CompilerParams(collective_id=0, has_side_effects=True),
    )(block, sent, weight, gain, w_in, w_out, scale)


def local(student, teacher, dw_weight, norm_gain, w_in, w_out, layer_scale):
    batch_size, tile_rows, tile_cols, channel_count = student.shape
    kernel_size = dw_weight.shape[0]
    lats = lax.axis_size("lat")
    cell_total = batch_size * tile_rows * lats * tile_cols * lax.axis_size("lon")
    sent = teacher.reshape(batch_size, lats, -1, teacher.shape[2], channel_count)
    sent = sent.transpose(1, 0, 2, 3, 4).reshape(lats, -1, channel_count)
    sum_in, sum_out, sum_dw, grad_student = whole_step(
        student, sent, dw_weight, norm_gain[None], w_in, w_out, layer_scale[None]
    )
    sum_dw = sum_dw[:, : kernel_size * TILE].reshape(2, kernel_size, TILE, SIDE)
    sum_dw = sum_dw[:, :, :kernel_size].transpose(1, 2, 0, 3)
    sum_dw = sum_dw.reshape(kernel_size, kernel_size, channel_count)
    return (
        grad_student,
        sum_in.astype(jnp.float32) / cell_total,
        sum_out.T.astype(jnp.float32) / cell_total,
        sum_dw / cell_total,
    )


def solution(mesh):
    placed = (
        P(None, "lat", "lon", None),
        P(None, None, ("lon", "lat"), None),
        P(),
        P(),
        P(),
        P(),
        P(),
    )
    return jax.shard_map(
        local,
        mesh=mesh,
        in_specs=placed,
        out_specs=(P(None, "lat", "lon", None), P(), P(), P()),
        check_vma=False,
    )
```

```python
import jax
import jax.numpy as jnp
from jax import lax
from jax.experimental import pallas as pl
from jax.experimental.pallas import tpu as pltpu
from jax.sharding import PartitionSpec as P

slope_coef = 0.7978845608028654
cubic_coef = 0.044715
norm_eps = 1e-06
MESH = pl.DeviceIdType.MESH

def start_remote(source, target, ssem, rsem, device_to):
    copy = pltpu.make_async_remote_copy(
        src_ref=source, dst_ref=target, send_sem=ssem, recv_sem=rsem,
        device_id=device_to, device_id_type=MESH,
    )
    copy.start()
    return copy


WIDTH = 3


def halo_friends(lat, lon, lats, lons):
    steps = [(0, 1), (0, -1), (1, 0), (-1, 0)]
    return [
        {"lat": lax.rem(lat + dl + lats, lats), "lon": lax.rem(lon + dn + lons, lons)}
        for dl, dn in steps
    ]


def halo_copies(block, edges, low, high, left, right, ssem, rsem):
    lats, lons = lax.axis_size("lat"), lax.axis_size("lon")
    lat, lon = lax.axis_index("lat"), lax.axis_index("lon")
    rows = block.shape[1]
    up = {"lat": jnp.minimum(lat + 1, lats - 1), "lon": lon}
    down = {"lat": jnp.maximum(lat - 1, 0), "lon": lon}
    first = lat == 0
    last = lat == lats - 1
    inner_up, inner_down = jnp.logical_not(last), jnp.logical_not(first)
    plan = [
        (edges.at[1], left.at[1], {"lat": lat, "lon": lax.rem(lon + 1, lons)}, None, None),
        (edges.at[0], right.at[1], {"lat": lat, "lon": lax.rem(lon + lons - 1, lons)}, None, None),
        (block.at[:, pl.ds(rows - WIDTH, WIDTH)], low, up, inner_up, inner_down),
        (block.at[:, pl.ds(0, WIDTH)], high, down, inner_down, inner_up),
        (left.at[1], left.at[0], up, inner_up, inner_down),
        (right.at[1], right.at[0], up, inner_up, inner_down),
        (left.at[1], left.at[2], down, inner_down, inner_up),
        (right.at[1], right.at[2], down, inner_down, inner_up),
    ]
    copies = []
    for k, (source, target, device_to, sends, comes) in enumerate(plan):
        copy = pltpu.make_async_remote_copy(
            src_ref=source, dst_ref=target, send_sem=ssem.at[k], recv_sem=rsem.at[k],
            device_id=device_to, device_id_type=MESH,
        )
        copies.append((copy, sends, comes))
    return copies


def run_if(condition, action):
    if condition is None:
        action()
    else:
        pl.when(condition)(action)


def halo_start(copies, low, high, left, right):
    lats, lat = lax.axis_size("lat"), lax.axis_index("lat")
    for copy, sends, _ in copies[:4]:
        run_if(sends, copy.start)

    @pl.when(lat == 0)
    def _():
        low[...] = jnp.zeros_like(low)
        left[0] = jnp.zeros(left.shape[1:], left.dtype)
        right[0] = jnp.zeros(right.shape[1:], right.dtype)

    @pl.when(lat == lats - 1)
    def _():
        high[...] = jnp.zeros_like(high)
        left[2] = jnp.zeros(left.shape[1:], left.dtype)
        right[2] = jnp.zeros(right.shape[1:], right.dtype)


def halo_pass_on(copies):
    for copy, _, _ in copies[:2]:
        copy.wait_recv()
    for copy, sends, _ in copies[4:]:
        run_if(sends, copy.start)


def halo_wait(copies):
    for k, (copy, sends, comes) in enumerate(copies):
        run_if(sends, copy.wait_send)
        if k >= 2:
            run_if(comes, copy.wait_recv)


def pack_edges(block, rows_f32, edges):
    batch, rows, cols, channels = block.shape
    for b in range(batch):
        for row in range(rows):
            at = (b * rows + row) * WIDTH
            line = block[b, row].astype(jnp.float32)
            rows_f32[0, at : at + WIDTH] = line[:WIDTH]
            rows_f32[1, at : at + WIDTH] = line[cols - WIDTH :]
    edges[...] = rows_f32[...].astype(edges.dtype)


def fill_padded(padded, edge_rows, block, low, high, left, right):
    batch, rows, cols, channels = block.shape
    for side, ref in enumerate((left, right)):
        for k in range(3):
            edge_rows[side, k] = ref[k].astype(jnp.float32)
    for b in range(batch):
        for row in range(rows + 2 * WIDTH):
            if row < WIDTH:
                line, k, r = low[b, row], 0, rows - WIDTH + row
            elif row < WIDTH + rows:
                line, k, r = block[b, row - WIDTH], 1, row - WIDTH
            else:
                line, k, r = high[b, row - WIDTH - rows], 2, row - WIDTH - rows
            at = (b * rows + r) * WIDTH
            padded[b, row, WIDTH : WIDTH + cols] = line.astype(jnp.float32)
            padded[b, row, :WIDTH] = edge_rows[0, k, at : at + WIDTH]
            padded[b, row, WIDTH + cols : 2 * WIDTH + cols] = edge_rows[1, k, at : at + WIDTH]


def run_stencil(padded, weight, shape, flipped, emit):
    batch, rows, cols, channels = shape
    size = weight.shape[0]

    @pl.loop(0, batch * rows)
    def _(n):
        b, row = n // rows, lax.rem(n, rows)
        total = jnp.zeros((cols, channels), jnp.float32)
        for p in range(size):
            for q in range(size):
                row_at = size - 1 - p if flipped else p
                col_at = size - 1 - q if flipped else q
                total = total + weight[p, q : q + 1] * padded[b, row + row_at, col_at : col_at + cols]
        emit(n, b, row, total)


def tap_sums(padded, cell_grad, shape, size, dw):
    batch, rows, cols, channels = shape
    dw[...] = jnp.zeros_like(dw)

    @pl.loop(0, size)
    def _(p):
        for q in range(size):
            total = jnp.zeros((TILE, channels), jnp.float32)
            for n in range(batch * rows):
                b, row = n // rows, n % rows
                product = padded[b, row + p, q : q + cols] * cell_grad[n * cols : (n + 1) * cols]
                for t in range(cols // TILE):
                    total = total + product[t * TILE : (t + 1) * TILE]
            line = jnp.sum(total, axis=0, keepdims=True)
            for half in range(2):
                dw[half, pl.ds(p * TILE + q, 1)] = line[:, half * SIDE : (half + 1) * SIDE]


BLOCKS, SIDE, SPLIT, TILE, DW_ROWS, DW_PAD = 16, 128, 64, 8, 4, 16
LOWER = SIDE - SPLIT + DW_PAD
CHIPS_Z = 16
CHUNK = 256


def block_slot(which, row, col):
    return row * 8 + col if which == 0 else row * 2 + col


def step_kernel(
    block, sent, weight, gain, w_in, w_out, scale,
    out_a, out_b, out_dw, out_grad_ref,
    edge_f32, edges, low, high, left, right, edge_rows, padded, came, came_f32, target,
    smoothed, unit, hid, slope, misfit, cell_grad, grad_block,
    edges2, low2h, high2h, left2h, right2h, padded2, dw_ref,
    own, other, dw_other, top, low_part, top_b, low_b, top_in1, low_in1, top1, low1, top_in2, low_in2,
    z_send, z_in, z_own, z_all, dw_send, dw_in, dw_sum_ref, dw_done, top_g1, low_g1, top_all, low_all,
    core_ssem, core_rsem, xy_ssem, xy_rsem, z_ssem, z_rsem, halo_ssem, halo_rsem,
    halo2_ssem, halo2_rsem, teach_ssem, teach_rsem, local_sem, dw_ssem, dw_rsem, pair_ssem, pair_rsem,
):
    f32, bf16 = jnp.float32, jnp.bfloat16
    lats, lons = lax.axis_size("lat"), lax.axis_size("lon")
    lat, lon = lax.axis_index("lat"), lax.axis_index("lon")
    core = lax.rem(lat, 2)
    z = lax.rem(lon, 2) * 8 + lat // 2
    x = lon // 8
    y = lax.rem(lon // 2, 4)

    def device(core_to, z_to, x_to, y_to):
        return {
            "lat": lax.rem(z_to, 8) * 2 + core_to,
            "lon": x_to * 8 + y_to * 2 + z_to // 8,
        }

    partner = device(1 - core, z, x, y)
    x_peers = [lax.rem(x + d, 4) for d in range(4)]
    y_peers = [lax.rem(y + d, 4) for d in range(4)]
    z_peers = [lax.rem(z + d, CHIPS_Z) for d in range(CHIPS_Z)]
    x_devices = [device(core, z, p, y) for p in x_peers]
    y_devices = [device(core, z, x, p) for p in y_peers]
    z_devices = [device(core, p, x, y) for p in z_peers]

    barrier = pltpu.get_barrier_semaphore()
    friends = [partner] + x_devices[1:] + y_devices[1:] + z_devices[1:]
    lat_peers = [lax.rem(lat + d, lats) for d in range(lats)]
    friends = friends + halo_friends(lat, lon, lats, lons)[:2]
    friends = friends + [{"lat": p, "lon": lon} for p in lat_peers[1:]]
    for friend in friends:
        pl.semaphore_signal(barrier, inc=1, device_id=friend, device_id_type=MESH)

    mine = pltpu.make_async_copy(sent.at[lat], came.at[lat], local_sem)
    mine.start()
    pack_edges(block, edge_f32, edges)
    pl.semaphore_wait(barrier, len(friends))

    front = halo_copies(block, edges, low, high, left, right, halo_ssem, halo_rsem)
    halo_start(front, low, high, left, right)
    teaching = [
        start_remote(
            sent.at[lat_peers[d]], came.at[lat], teach_ssem.at[d], teach_rsem.at[d],
            {"lat": lat_peers[d], "lon": lon},
        )
        for d in range(1, lats)
    ]
    halo_pass_on(front)
    halo_wait(front)
    fill_padded(padded, edge_rows, block, low, high, left, right)

    shape = block.shape
    batch, rows, cols, channels = shape

    def keep(n, b, row, total):
        smoothed[pl.ds(pl.multiple_of(n * cols, cols), cols)] = total

    run_stencil(padded, weight, shape, False, keep)
    smooth = smoothed[...]
    average = jnp.mean(smooth, axis=-1, keepdims=True)
    centred = smooth - average
    variance = jnp.mean(centred * centred, axis=-1, keepdims=True)
    inv_std = lax.rsqrt(variance + norm_eps)
    unit[...] = centred * inv_std
    normed = (unit[...] * gain[...]).astype(bf16)
    mlp_out = jnp.zeros((batch * rows * cols, channels), f32)
    hidden_size = w_in.shape[1]
    for at in range(0, hidden_size, CHUNK):
        preact = jnp.dot(normed, w_in[:, at : at + CHUNK], preferred_element_type=f32)
        tangent = jnp.tanh(slope_coef * (preact + cubic_coef * preact * preact * preact))
        hidden = (0.5 * preact * (1.0 + tangent)).astype(bf16)
        hid[:, at : at + CHUNK] = hidden
        slope[:, at : at + CHUNK] = 0.5 * (1.0 + tangent) + 0.5 * preact * (
            1.0 - tangent * tangent
        ) * slope_coef * (1.0 + 3.0 * cubic_coef * preact * preact)
        mlp_out = mlp_out + jnp.dot(hidden, w_out[at : at + CHUNK], preferred_element_type=f32)

    mine.wait()
    for copy in teaching:
        copy.wait()
    for src in range(lats):
        came_f32[src] = came[src].astype(f32)
    part = cols // lats
    for src in range(lats):
        for n in range(batch * rows):
            at = n * cols + src * part
            target[at : at + part] = came_f32[src, n * part : (n + 1) * part]
    student = jnp.concatenate(
        [block[n // rows, n % rows] for n in range(batch * rows)], axis=0
    ).astype(f32)
    misfit[...] = (student + scale[...] * mlp_out) - target[...]
    out_grad = (scale[...] * misfit[...]).astype(bf16)
    contract_cells = (((0,), (0,)), ((), ()))
    contract_last = (((1,), (1,)), ((), ()))

    def keep_product(which, row_at, col_at, product):
        for row in range(product.shape[0] // SIDE):
            for col in range(product.shape[1] // SIDE):
                slot = block_slot(which, row_at // SIDE + row, col_at // SIDE + col)
                own[which, slot] = product[
                    row * SIDE : (row + 1) * SIDE, col * SIDE : (col + 1) * SIDE
                ]

    normed_grad = jnp.zeros((batch * rows * cols, channels), f32)
    for at in range(0, hidden_size, CHUNK):
        hidden_grad = lax.dot_general(
            out_grad, w_out[at : at + CHUNK], contract_last, preferred_element_type=f32
        )
        preact_grad = (hidden_grad * slope[:, at : at + CHUNK]).astype(bf16)
        keep_product(
            0, 0, at, lax.dot_general(normed, preact_grad, contract_cells, preferred_element_type=f32)
        )
        keep_product(
            1,
            at,
            0,
            lax.dot_general(
                hid[:, at : at + CHUNK], out_grad, contract_cells, preferred_element_type=f32
            ),
        )
        normed_grad = normed_grad + lax.dot_general(
            preact_grad, w_in[:, at : at + CHUNK], contract_last, preferred_element_type=f32
        )
    core_copies = [
        start_remote(own.at[1 - core], other, core_ssem.at[0], core_rsem.at[0], partner)
    ]
    unit_grad = normed_grad * gain[...]
    unit_norm = unit[...]
    first_mean = jnp.mean(unit_grad, axis=-1, keepdims=True)
    second_mean = jnp.mean(unit_grad * unit_norm, axis=-1, keepdims=True)
    conv_grad = (inv_std * (unit_grad - first_mean - unit_norm * second_mean)).astype(bf16)
    for n in range(batch * rows):
        grad_block[n // rows, n % rows] = conv_grad[n * cols : (n + 1) * cols]
    cell_grad[...] = conv_grad.astype(f32)
    pack_edges(grad_block, edge_f32, edges2)
    halo = halo_copies(
        grad_block, edges2, low2h, high2h, left2h, right2h, halo2_ssem, halo2_rsem
    )
    halo_start(halo, low2h, high2h, left2h, right2h)
    tap_sums(padded, cell_grad, shape, weight.shape[0], dw_ref)
    copies = core_copies + [
        start_remote(dw_ref.at[1 - core], dw_other, core_ssem.at[1], core_rsem.at[1], partner),
    ]
    for copy in copies:
        copy.wait()
    for block in range(BLOCKS):
        bx, by = block // 4, block % 4
        top[bx, by] = own[core, block, :SPLIT] + other[block, :SPLIT]
        low_part[by, bx, : SIDE - SPLIT] = own[core, block, SPLIT:] + other[block, SPLIT:]
        rows = slice(DW_ROWS * block, DW_ROWS * (block + 1))
        dw_sum = dw_ref[core, rows] + dw_other[rows]
        low_part[by, bx, SIDE - SPLIT :] = jnp.concatenate(
            [dw_sum, jnp.zeros((DW_PAD - DW_ROWS, SIDE), jnp.float32)], axis=0
        )

    for k in range(4):
        top_b[k] = top[k].astype(bf16)
        low_b[k] = low_part[k].astype(bf16)
    copies = []
    for d in (2, 1, 3):
        copies.append(
            start_remote(top_b.at[x_peers[d]], top_in1.at[d], xy_ssem.at[0, d], xy_rsem.at[0, d], x_devices[d])
        )
        copies.append(
            start_remote(low_b.at[y_peers[d]], low_in1.at[d], xy_ssem.at[1, d], xy_rsem.at[1, d], y_devices[d])
        )
    for copy in copies:
        copy.wait()
    top1[...] = top[x] + top_in1[1].astype(f32) + top_in1[2].astype(f32) + top_in1[3].astype(f32)
    low1[...] = (
        low_part[y] + low_in1[1].astype(f32) + low_in1[2].astype(f32) + low_in1[3].astype(f32)
    )

    copies = []
    for d in (2, 1, 3):
        copies.append(
            start_remote(top1.at[y_peers[d]], top_in2.at[d], xy_ssem.at[2, d], xy_rsem.at[2, d], y_devices[d])
        )
        copies.append(
            start_remote(low1.at[x_peers[d]], low_in2.at[d], xy_ssem.at[3, d], xy_rsem.at[3, d], x_devices[d])
        )
    for copy in copies:
        copy.wait()
    top2 = top1[y] + top_in2[1] + top_in2[2] + top_in2[3]
    low2 = low1[x] + low_in2[1] + low_in2[2] + low_in2[3]
    for tile in range(CHIPS_Z):
        at = TILE * tile
        z_send[tile] = top2[at : at + TILE] if at < SPLIT else low2[at - SPLIT : at - SPLIT + TILE]
    dw_send[...] = low2[SIDE - SPLIT : SIDE - SPLIT + TILE]

    order = [8, 7, 9, 6, 10, 5, 11, 4, 12, 3, 13, 2, 14, 1, 15]
    copies = []
    for d in order:
        copies.append(
            start_remote(z_send.at[z_peers[d]], z_in.at[z], z_ssem.at[0, d], z_rsem.at[0, d], z_devices[d])
        )
    owner = x * 4 + y
    is_owner = z == owner
    toward = lax.rem(owner - z + CHIPS_Z, CHIPS_Z)
    away = lax.rem(z - owner + CHIPS_Z, CHIPS_Z)
    dw_copy = pltpu.make_async_remote_copy(
        src_ref=dw_send, dst_ref=dw_in.at[z], send_sem=dw_ssem.at[0], recv_sem=dw_rsem.at[0, toward],
        device_id=device(core, owner, x, y), device_id_type=MESH,
    )
    pl.when(jnp.logical_not(is_owner))(dw_copy.start)

    @pl.when(is_owner)
    def _():
        dw_in[z] = dw_send[...]

    z_in[z] = z_send[z]
    halo_pass_on(halo)
    for copy in copies:
        copy.wait()
    total = z_in[0]
    for tile in range(1, CHIPS_Z):
        total = total + z_in[tile]
    z_own[...] = total

    def dw_spread(d):
        return pltpu.make_async_remote_copy(
            src_ref=dw_sum_ref, dst_ref=dw_done, send_sem=dw_ssem.at[d], recv_sem=dw_rsem.at[1, d],
            device_id=z_devices[d], device_id_type=MESH,
        )

    @pl.when(is_owner)
    def _():
        for d in range(1, CHIPS_Z):
            pltpu.make_async_remote_copy(
                src_ref=dw_send, dst_ref=dw_in.at[z], send_sem=dw_ssem.at[0],
                recv_sem=dw_rsem.at[0, d], device_id=partner, device_id_type=MESH,
            ).wait_recv()
        dw_total = dw_in[0]
        for tile in range(1, CHIPS_Z):
            dw_total = dw_total + dw_in[tile]
        dw_sum_ref[...] = dw_total
        for d in order:
            dw_spread(d).start()
        dw_done[...] = dw_total

    copies = []
    for d in order:
        copies.append(
            start_remote(z_own, z_all.at[z], z_ssem.at[1, d], z_rsem.at[1, d], z_devices[d])
        )
    z_all[z] = z_own[...]
    halo_wait(halo)
    fill_padded(padded2, edge_rows, grad_block, low2h, high2h, left2h, right2h)

    def finish(n, b, row, total):
        cells = pl.ds(pl.multiple_of(n * cols, cols), cols)
        out_grad_ref[b, row] = (misfit[cells] + total).astype(bf16)

    run_stencil(padded2, weight, shape, True, finish)

    @pl.when(is_owner)
    def _():
        for d in range(1, CHIPS_Z):
            dw_spread(d).wait_send()

    @pl.when(jnp.logical_not(is_owner))
    def _():
        dw_copy.wait_send()
        pltpu.make_async_remote_copy(
            src_ref=dw_sum_ref, dst_ref=dw_done, send_sem=dw_ssem.at[0],
            recv_sem=dw_rsem.at[1, away], device_id=partner, device_id_type=MESH,
        ).wait_recv()

    for copy in copies:
        copy.wait()
    tiles = z_all[...].reshape(SIDE, SIDE)
    dw_tile = jnp.concatenate(
        [dw_done[...], jnp.zeros((DW_PAD - TILE, SIDE), jnp.float32)], axis=0
    )
    top_g1[y] = tiles[:SPLIT].astype(jnp.bfloat16)
    low_g1[x] = jnp.concatenate([tiles[SPLIT:], dw_tile], axis=0).astype(jnp.bfloat16)

    copies = []
    for d in (2, 1, 3):
        copies.append(
            start_remote(top_g1.at[y], top_g1.at[y], xy_ssem.at[4, d], xy_rsem.at[4, d], y_devices[d])
        )
        copies.append(
            start_remote(low_g1.at[x], low_g1.at[x], xy_ssem.at[5, d], xy_rsem.at[5, d], x_devices[d])
        )
    for copy in copies:
        copy.wait()

    copies = []
    for d in (2, 1, 3):
        copies.append(
            start_remote(top_g1, top_all.at[core, x], xy_ssem.at[6, d], xy_rsem.at[6, d], x_devices[d])
        )
        copies.append(
            start_remote(low_g1, low_all.at[core, y], xy_ssem.at[7, d], xy_rsem.at[7, d], y_devices[d])
        )
    top_all[core, x] = top_g1[...]
    low_all[core, y] = low_g1[...]
    core_copies = []

    def to_partner(buffer, slot, k, part):
        core_copies.append(
            start_remote(
                buffer.at[core, slot], buffer.at[core, slot], pair_ssem.at[part, k],
                pair_rsem.at[part, k], partner,
            )
        )

    to_partner(top_all, x, 0, 0)
    to_partner(low_all, y, 0, 1)
    for k, d in ((2, 1), (3, 1), (4, 3), (5, 3), (0, 2), (1, 2)):
        copies[k].wait_recv()
        if k % 2 == 0:
            to_partner(top_all, lax.rem(x - d + 4, 4), d, 0)
        else:
            to_partner(low_all, lax.rem(y - d + 4, 4), d, 1)
    for copy in copies:
        copy.wait_send()
    for copy in core_copies:
        copy.wait()
    for which, out in enumerate((out_a, out_b)):
        for block in range(BLOCKS):
            bx, by = block // 4, block % 4
            across_blocks = 8 if which == 0 else 2
            row, col = SIDE * (block // across_blocks), SIDE * (block % across_blocks)
            out[row : row + SPLIT, col : col + SIDE] = top_all[which, bx, by]
            out[row + SPLIT : row + SIDE, col : col + SIDE] = low_all[which, by, bx, : SIDE - SPLIT]
            dw_rows = low_all[which, by, bx, SIDE - SPLIT :].astype(jnp.float32)[:DW_ROWS]
            out_dw[which, DW_ROWS * block : DW_ROWS * (block + 1)] = dw_rows


def whole_step(block, sent, weight, gain, w_in, w_out, scale):
    f32, bf16 = jnp.float32, jnp.bfloat16
    batch, rows, cols, channels = block.shape
    cells, lats = batch * rows * cols, sent.shape[0]
    edge_cells = batch * rows * WIDTH
    vmem = pl.BlockSpec(memory_space=pltpu.VMEM)
    across = pltpu.VMEM((batch, WIDTH, cols, channels), bf16)
    along = pltpu.VMEM((3, edge_cells, channels), bf16)
    padded = pltpu.VMEM((batch, rows + 2 * WIDTH, cols + 2 * WIDTH + 2, channels), f32)
    dw_shape = (2, BLOCKS * DW_ROWS, SIDE)
    cell_f32 = pltpu.VMEM((cells, channels), f32)
    return pl.pallas_call(
        step_kernel,
        out_shape=(
            jax.ShapeDtypeStruct(w_in.shape, bf16),
            jax.ShapeDtypeStruct(w_out.shape, bf16),
            jax.ShapeDtypeStruct(dw_shape, f32),
            jax.ShapeDtypeStruct(block.shape, bf16),
        ),
        in_specs=[vmem] * 7,
        out_specs=(vmem,) * 4,
        scratch_shapes=[
            pltpu.VMEM((2, edge_cells, channels), f32),
            pltpu.VMEM((2, edge_cells, channels), bf16),
            across,
            across,
            along,
            along,
            pltpu.VMEM((2, 3, edge_cells, channels), f32),
            padded,
            pltpu.VMEM(sent.shape, bf16),
            pltpu.VMEM(sent.shape, f32),
            cell_f32,
            cell_f32,
            cell_f32,
            pltpu.VMEM((cells, w_in.shape[1]), bf16),
            pltpu.VMEM((cells, w_in.shape[1]), f32),
            cell_f32,
            cell_f32,
            pltpu.VMEM(block.shape, bf16),
            pltpu.VMEM((2, edge_cells, channels), bf16),
            across,
            across,
            along,
            along,
            padded,
            pltpu.VMEM(dw_shape, f32),
            pltpu.VMEM((2, BLOCKS, SIDE, SIDE), f32),
            pltpu.VMEM((BLOCKS, SIDE, SIDE), f32),
            pltpu.VMEM(dw_shape[1:], f32),
            pltpu.VMEM((4, 4, SPLIT, SIDE), f32),
            pltpu.VMEM((4, 4, LOWER, SIDE), f32),
            pltpu.VMEM((4, 4, SPLIT, SIDE), bf16),
            pltpu.VMEM((4, 4, LOWER, SIDE), bf16),
            pltpu.VMEM((4, 4, SPLIT, SIDE), bf16),
            pltpu.VMEM((4, 4, LOWER, SIDE), bf16),
            pltpu.VMEM((4, SPLIT, SIDE), f32),
            pltpu.VMEM((4, LOWER, SIDE), f32),
            pltpu.VMEM((4, SPLIT, SIDE), f32),
            pltpu.VMEM((4, LOWER, SIDE), f32),
            pltpu.VMEM((CHIPS_Z, TILE, SIDE), f32),
            pltpu.VMEM((CHIPS_Z, TILE, SIDE), f32),
            pltpu.VMEM((TILE, SIDE), f32),
            pltpu.VMEM((CHIPS_Z, TILE, SIDE), f32),
            pltpu.VMEM((TILE, SIDE), f32),
            pltpu.VMEM((CHIPS_Z, TILE, SIDE), f32),
            pltpu.VMEM((TILE, SIDE), f32),
            pltpu.VMEM((TILE, SIDE), f32),
            pltpu.VMEM((4, SPLIT, SIDE), bf16),
            pltpu.VMEM((4, LOWER, SIDE), bf16),
            pltpu.VMEM((2, 4, 4, SPLIT, SIDE), bf16),
            pltpu.VMEM((2, 4, 4, LOWER, SIDE), bf16),
            pltpu.SemaphoreType.DMA((4,)),
            pltpu.SemaphoreType.DMA((4,)),
            pltpu.SemaphoreType.DMA((8, 4)),
            pltpu.SemaphoreType.DMA((8, 4)),
            pltpu.SemaphoreType.DMA((2, CHIPS_Z)),
            pltpu.SemaphoreType.DMA((2, CHIPS_Z)),
            pltpu.SemaphoreType.DMA((8,)),
            pltpu.SemaphoreType.DMA((8,)),
            pltpu.SemaphoreType.DMA((8,)),
            pltpu.SemaphoreType.DMA((8,)),
            pltpu.SemaphoreType.DMA((lats,)),
            pltpu.SemaphoreType.DMA((lats,)),
            pltpu.SemaphoreType.DMA,
            pltpu.SemaphoreType.DMA((CHIPS_Z,)),
            pltpu.SemaphoreType.DMA((2, CHIPS_Z)),
            pltpu.SemaphoreType.DMA((2, 4)),
            pltpu.SemaphoreType.DMA((2, 4)),
        ],
        compiler_params=pltpu.CompilerParams(collective_id=0, has_side_effects=True),
    )(block, sent, weight, gain, w_in, w_out, scale)


def local(student, teacher, dw_weight, norm_gain, w_in, w_out, layer_scale):
    batch_size, tile_rows, tile_cols, channel_count = student.shape
    kernel_size = dw_weight.shape[0]
    lats = lax.axis_size("lat")
    cell_total = batch_size * tile_rows * lats * tile_cols * lax.axis_size("lon")
    sent = teacher.reshape(batch_size, lats, -1, teacher.shape[2], channel_count)
    sent = sent.transpose(1, 0, 2, 3, 4).reshape(lats, -1, channel_count)
    sum_in, sum_out, sum_dw, grad_student = whole_step(
        student, sent, dw_weight, norm_gain[None], w_in, w_out, layer_scale[None]
    )
    sum_dw = sum_dw[:, : kernel_size * TILE].reshape(2, kernel_size, TILE, SIDE)
    sum_dw = sum_dw[:, :, :kernel_size].transpose(1, 2, 0, 3)
    sum_dw = sum_dw.reshape(kernel_size, kernel_size, channel_count)
    return (
        grad_student,
        sum_in.astype(jnp.float32) / cell_total,
        sum_out.astype(jnp.float32) / cell_total,
        sum_dw / cell_total,
    )


def solution(mesh):
    placed = (
        P(None, "lat", "lon", None),
        P(None, None, ("lon", "lat"), None),
        P(),
        P(),
        P(),
        P(),
        P(),
    )
    return jax.shard_map(
        local,
        mesh=mesh,
        in_specs=placed,
        out_specs=(P(None, "lat", "lon", None), P(), P(), P()),
        check_vma=False,
    )
```

```python
import jax
import jax.numpy as jnp
from jax import lax
from jax.experimental import pallas as pl
from jax.experimental.pallas import tpu as pltpu
from jax.sharding import PartitionSpec as P

slope_coef = 0.7978845608028654
cubic_coef = 0.044715
norm_eps = 1e-06
MESH = pl.DeviceIdType.MESH

def start_remote(source, target, ssem, rsem, device_to):
    copy = pltpu.make_async_remote_copy(
        src_ref=source, dst_ref=target, send_sem=ssem, recv_sem=rsem,
        device_id=device_to, device_id_type=MESH,
    )
    copy.start()
    return copy


WIDTH = 3


def halo_friends(lat, lon, lats, lons):
    steps = [(0, 1), (0, -1), (1, 0), (-1, 0)]
    return [
        {"lat": lax.rem(lat + dl + lats, lats), "lon": lax.rem(lon + dn + lons, lons)}
        for dl, dn in steps
    ]


def halo_copies(block, edges, low, high, left, right, ssem, rsem):
    lats, lons = lax.axis_size("lat"), lax.axis_size("lon")
    lat, lon = lax.axis_index("lat"), lax.axis_index("lon")
    rows = block.shape[1]
    up = {"lat": jnp.minimum(lat + 1, lats - 1), "lon": lon}
    down = {"lat": jnp.maximum(lat - 1, 0), "lon": lon}
    first = lat == 0
    last = lat == lats - 1
    inner_up, inner_down = jnp.logical_not(last), jnp.logical_not(first)
    plan = [
        (edges.at[1], left.at[1], {"lat": lat, "lon": lax.rem(lon + 1, lons)}, None, None),
        (edges.at[0], right.at[1], {"lat": lat, "lon": lax.rem(lon + lons - 1, lons)}, None, None),
        (block.at[:, pl.ds(rows - WIDTH, WIDTH)], low, up, inner_up, inner_down),
        (block.at[:, pl.ds(0, WIDTH)], high, down, inner_down, inner_up),
        (left.at[1], left.at[0], up, inner_up, inner_down),
        (right.at[1], right.at[0], up, inner_up, inner_down),
        (left.at[1], left.at[2], down, inner_down, inner_up),
        (right.at[1], right.at[2], down, inner_down, inner_up),
    ]
    copies = []
    for k, (source, target, device_to, sends, comes) in enumerate(plan):
        copy = pltpu.make_async_remote_copy(
            src_ref=source, dst_ref=target, send_sem=ssem.at[k], recv_sem=rsem.at[k],
            device_id=device_to, device_id_type=MESH,
        )
        copies.append((copy, sends, comes))
    return copies


def run_if(condition, action):
    if condition is None:
        action()
    else:
        pl.when(condition)(action)


def halo_start(copies, low, high, left, right):
    lats, lat = lax.axis_size("lat"), lax.axis_index("lat")
    for copy, sends, _ in copies[:4]:
        run_if(sends, copy.start)

    @pl.when(lat == 0)
    def _():
        low[...] = jnp.zeros_like(low)
        left[0] = jnp.zeros(left.shape[1:], left.dtype)
        right[0] = jnp.zeros(right.shape[1:], right.dtype)

    @pl.when(lat == lats - 1)
    def _():
        high[...] = jnp.zeros_like(high)
        left[2] = jnp.zeros(left.shape[1:], left.dtype)
        right[2] = jnp.zeros(right.shape[1:], right.dtype)


def halo_pass_on(copies):
    for copy, _, _ in copies[:2]:
        copy.wait_recv()
    for copy, sends, _ in copies[4:]:
        run_if(sends, copy.start)


def halo_wait(copies):
    for k, (copy, sends, comes) in enumerate(copies):
        run_if(sends, copy.wait_send)
        if k >= 2:
            run_if(comes, copy.wait_recv)


def pack_edges(block, rows_f32, edges):
    batch, rows, cols, channels = block.shape
    for b in range(batch):
        for row in range(rows):
            at = (b * rows + row) * WIDTH
            line = block[b, row].astype(jnp.float32)
            rows_f32[0, at : at + WIDTH] = line[:WIDTH]
            rows_f32[1, at : at + WIDTH] = line[cols - WIDTH :]
    edges[...] = rows_f32[...].astype(edges.dtype)


def fill_padded(padded, edge_rows, block, low, high, left, right):
    batch, rows, cols, channels = block.shape
    for side, ref in enumerate((left, right)):
        for k in range(3):
            edge_rows[side, k] = ref[k].astype(jnp.float32)
    for b in range(batch):
        for row in range(rows + 2 * WIDTH):
            if row < WIDTH:
                line, k, r = low[b, row], 0, rows - WIDTH + row
            elif row < WIDTH + rows:
                line, k, r = block[b, row - WIDTH], 1, row - WIDTH
            else:
                line, k, r = high[b, row - WIDTH - rows], 2, row - WIDTH - rows
            at = (b * rows + r) * WIDTH
            padded[b, row, WIDTH : WIDTH + cols] = line.astype(jnp.float32)
            padded[b, row, :WIDTH] = edge_rows[0, k, at : at + WIDTH]
            padded[b, row, WIDTH + cols : 2 * WIDTH + cols] = edge_rows[1, k, at : at + WIDTH]


def run_stencil(padded, weight, shape, flipped, emit):
    batch, rows, cols, channels = shape
    size = weight.shape[0]

    @pl.loop(0, batch * rows)
    def _(n):
        b, row = n // rows, lax.rem(n, rows)
        total = jnp.zeros((cols, channels), jnp.float32)
        for p in range(size):
            for q in range(size):
                row_at = size - 1 - p if flipped else p
                col_at = size - 1 - q if flipped else q
                total = total + weight[p, q : q + 1] * padded[b, row + row_at, col_at : col_at + cols]
        emit(n, b, row, total)


def tap_sums(padded, cell_grad, shape, size, dw):
    batch, rows, cols, channels = shape
    dw[...] = jnp.zeros_like(dw)

    @pl.loop(0, size)
    def _(p):
        for q in range(size):
            total = jnp.zeros((TILE, channels), jnp.float32)
            for n in range(batch * rows):
                b, row = n // rows, n % rows
                product = padded[b, row + p, q : q + cols] * cell_grad[n * cols : (n + 1) * cols]
                for t in range(cols // TILE):
                    total = total + product[t * TILE : (t + 1) * TILE]
            line = jnp.sum(total, axis=0, keepdims=True)
            for half in range(2):
                dw[half, pl.ds(p * TILE + q, 1)] = line[:, half * SIDE : (half + 1) * SIDE]


BLOCKS, SIDE, SPLIT, TILE, DW_ROWS, DW_PAD = 16, 128, 64, 8, 4, 16
REST = SIDE - SPLIT
LOWER = REST + DW_PAD
CHIPS_Z = 16
CHUNK = 256


def block_slot(which, row, col):
    return row * 8 + col if which == 0 else row * 2 + col


def step_kernel(
    block, sent, weight, gain, w_in, w_out, scale,
    out_a, out_b, out_dw, out_grad_ref,
    edge_f32, edges, low, high, left, right, edge_rows, padded, came, came_f32, target,
    smoothed, unit, hid, slope, misfit, cell_grad, grad_block,
    edges2, low2h, high2h, left2h, right2h, padded2, dw_ref,
    own, other, dw_other, top, low_part, top_b, low_b, top_in1, low_in1, top1, low1, top_in2, low_in2,
    z_send, z_in, z_own, z_all, dw_send, dw_in, dw_sum_ref, dw_done, dw_parts, dw_xy, top_g1, low_g1, top_all, low_all,
    core_ssem, core_rsem, xy_ssem, xy_rsem, z_ssem, z_rsem, halo_ssem, halo_rsem,
    halo2_ssem, halo2_rsem, teach_ssem, teach_rsem, local_sem, dw_ssem, dw_rsem, dw_xy_ssem, dw_xy_rsem, pair_ssem, pair_rsem,
):
    f32, bf16 = jnp.float32, jnp.bfloat16
    lats, lons = lax.axis_size("lat"), lax.axis_size("lon")
    cell_total = block.shape[0] * block.shape[1] * block.shape[2] * lats * lons
    lat, lon = lax.axis_index("lat"), lax.axis_index("lon")
    core = lax.rem(lat, 2)
    z = lax.rem(lon, 2) * 8 + lat // 2
    x = lon // 8
    y = lax.rem(lon // 2, 4)

    def device(core_to, z_to, x_to, y_to):
        return {
            "lat": lax.rem(z_to, 8) * 2 + core_to,
            "lon": x_to * 8 + y_to * 2 + z_to // 8,
        }

    partner = device(1 - core, z, x, y)
    x_peers = [lax.rem(x + d, 4) for d in range(4)]
    y_peers = [lax.rem(y + d, 4) for d in range(4)]
    z_peers = [lax.rem(z + d, CHIPS_Z) for d in range(CHIPS_Z)]
    x_devices = [device(core, z, p, y) for p in x_peers]
    y_devices = [device(core, z, x, p) for p in y_peers]
    z_devices = [device(core, p, x, y) for p in z_peers]

    barrier = pltpu.get_barrier_semaphore()
    friends = [partner] + x_devices[1:] + y_devices[1:] + z_devices[1:]
    diagonal = [(dx, dy) for dx in range(1, 4) for dy in range(1, 4)]
    friends = friends + [device(core, z, x_peers[dx], y_peers[dy]) for dx, dy in diagonal]
    lat_peers = [lax.rem(lat + d, lats) for d in range(lats)]
    friends = friends + halo_friends(lat, lon, lats, lons)[:2]
    friends = friends + [{"lat": p, "lon": lon} for p in lat_peers[1:]]
    for friend in friends:
        pl.semaphore_signal(barrier, inc=1, device_id=friend, device_id_type=MESH)

    mine = pltpu.make_async_copy(sent.at[:, pl.ds(lat * block.shape[1], block.shape[1])], came.at[lat], local_sem)
    mine.start()
    pack_edges(block, edge_f32, edges)
    pl.semaphore_wait(barrier, len(friends))

    front = halo_copies(block, edges, low, high, left, right, halo_ssem, halo_rsem)
    halo_start(front, low, high, left, right)
    teaching = [
        start_remote(
            sent.at[:, pl.ds(lat_peers[d] * block.shape[1], block.shape[1])], came.at[lat], teach_ssem.at[d], teach_rsem.at[d],
            {"lat": lat_peers[d], "lon": lon},
        )
        for d in range(1, lats)
    ]
    halo_pass_on(front)
    halo_wait(front)
    fill_padded(padded, edge_rows, block, low, high, left, right)

    shape = block.shape
    batch, rows, cols, channels = shape

    def keep(n, b, row, total):
        smoothed[pl.ds(pl.multiple_of(n * cols, cols), cols)] = total

    run_stencil(padded, weight, shape, False, keep)
    smooth = smoothed[...]
    average = jnp.mean(smooth, axis=-1, keepdims=True)
    centred = smooth - average
    variance = jnp.mean(centred * centred, axis=-1, keepdims=True)
    inv_std = lax.rsqrt(variance + norm_eps)
    unit[...] = centred * inv_std
    normed = (unit[...] * gain[...]).astype(bf16)
    mlp_out = jnp.zeros((batch * rows * cols, channels), f32)
    hidden_size = w_in.shape[1]
    for at in range(0, hidden_size, CHUNK):
        preact = jnp.dot(normed, w_in[:, at : at + CHUNK], preferred_element_type=f32)
        tangent = jnp.tanh(slope_coef * (preact + cubic_coef * preact * preact * preact))
        hidden = (0.5 * preact * (1.0 + tangent)).astype(bf16)
        hid[:, at : at + CHUNK] = hidden
        slope[:, at : at + CHUNK] = 0.5 * (1.0 + tangent) + 0.5 * preact * (
            1.0 - tangent * tangent
        ) * slope_coef * (1.0 + 3.0 * cubic_coef * preact * preact)
        mlp_out = mlp_out + jnp.dot(hidden, w_out[at : at + CHUNK], preferred_element_type=f32)

    mine.wait()
    for copy in teaching:
        copy.wait()
    for src in range(lats):
        for n in range(batch * rows):
            came_f32[src, n] = came[src, n // rows, n % rows].astype(f32)
    part = cols // lats
    for src in range(lats):
        for n in range(batch * rows):
            at = n * cols + src * part
            target[at : at + part] = came_f32[src, n]
    student = jnp.concatenate(
        [block[n // rows, n % rows] for n in range(batch * rows)], axis=0
    ).astype(f32)
    misfit[...] = (student + scale[...] * mlp_out) - target[...]
    out_grad = (scale[...] * misfit[...]).astype(bf16)
    contract_cells = (((0,), (0,)), ((), ()))
    contract_last = (((1,), (1,)), ((), ()))

    def keep_product(which, row_at, col_at, product):
        for row in range(product.shape[0] // SIDE):
            for col in range(product.shape[1] // SIDE):
                slot = block_slot(which, row_at // SIDE + row, col_at // SIDE + col)
                own[which, slot] = product[
                    row * SIDE : (row + 1) * SIDE, col * SIDE : (col + 1) * SIDE
                ]

    normed_grad = jnp.zeros((batch * rows * cols, channels), f32)
    for at in range(0, hidden_size, CHUNK):
        hidden_grad = lax.dot_general(
            out_grad, w_out[at : at + CHUNK], contract_last, preferred_element_type=f32
        )
        preact_grad = (hidden_grad * slope[:, at : at + CHUNK]).astype(bf16)
        keep_product(
            0, 0, at, lax.dot_general(normed, preact_grad, contract_cells, preferred_element_type=f32)
        )
        keep_product(
            1,
            at,
            0,
            lax.dot_general(
                hid[:, at : at + CHUNK], out_grad, contract_cells, preferred_element_type=f32
            ),
        )
        normed_grad = normed_grad + lax.dot_general(
            preact_grad, w_in[:, at : at + CHUNK], contract_last, preferred_element_type=f32
        )
    core_copies = [
        start_remote(own.at[1 - core], other, core_ssem.at[0], core_rsem.at[0], partner)
    ]
    unit_grad = normed_grad * gain[...]
    unit_norm = unit[...]
    first_mean = jnp.mean(unit_grad, axis=-1, keepdims=True)
    second_mean = jnp.mean(unit_grad * unit_norm, axis=-1, keepdims=True)
    conv_grad = (inv_std * (unit_grad - first_mean - unit_norm * second_mean)).astype(bf16)
    for n in range(batch * rows):
        grad_block[n // rows, n % rows] = conv_grad[n * cols : (n + 1) * cols]
    cell_grad[...] = conv_grad.astype(f32)
    pack_edges(grad_block, edge_f32, edges2)
    halo = halo_copies(
        grad_block, edges2, low2h, high2h, left2h, right2h, halo2_ssem, halo2_rsem
    )
    halo_start(halo, low2h, high2h, left2h, right2h)
    tap_sums(padded, cell_grad, shape, weight.shape[0], dw_ref)
    dw_core = start_remote(
        dw_ref.at[1 - core], dw_other, core_ssem.at[1], core_rsem.at[1], partner
    )
    for copy in core_copies:
        copy.wait()
    for block in range(BLOCKS):
        bx, by = block // 4, block % 4
        top[bx, by] = own[core, block, :SPLIT] + other[block, :SPLIT]
        low_part[by, bx] = own[core, block, SPLIT:] + other[block, SPLIT:]

    for k in range(4):
        top_b[k] = top[k].astype(bf16)
        low_b[k] = low_part[k].astype(bf16)
    copies = []
    for d in (2, 1, 3):
        copies.append(
            start_remote(top_b.at[x_peers[d]], top_in1.at[d], xy_ssem.at[0, d], xy_rsem.at[0, d], x_devices[d])
        )
        copies.append(
            start_remote(low_b.at[y_peers[d]], low_in1.at[d], xy_ssem.at[1, d], xy_rsem.at[1, d], y_devices[d])
        )
    dw_core.wait()
    group = x * 4 + y
    for slot in range(BLOCKS):
        lines = slice(DW_ROWS * slot, DW_ROWS * (slot + 1))
        dw_parts[slot, :DW_ROWS] = dw_ref[core, lines] + dw_other[lines]
        dw_parts[slot, DW_ROWS:] = jnp.zeros((TILE - DW_ROWS, SIDE), f32)
    dw_copies = []
    for k in range(1, BLOCKS):
        px, py = x_peers[k // 4], y_peers[k % 4]
        dw_copies.append(
            start_remote(
                dw_parts.at[px * 4 + py], dw_xy.at[group], dw_xy_ssem.at[k], dw_xy_rsem.at[k],
                device(core, z, px, py),
            )
        )
    dw_xy[group] = dw_parts[group]
    for copy in copies:
        copy.wait()
    top1[...] = top[x] + top_in1[1].astype(f32) + top_in1[2].astype(f32) + top_in1[3].astype(f32)
    low1[...] = (
        low_part[y] + low_in1[1].astype(f32) + low_in1[2].astype(f32) + low_in1[3].astype(f32)
    )

    copies = []
    for d in (2, 1, 3):
        copies.append(
            start_remote(top1.at[y_peers[d]], top_in2.at[d], xy_ssem.at[2, d], xy_rsem.at[2, d], y_devices[d])
        )
        copies.append(
            start_remote(low1.at[x_peers[d]], low_in2.at[d], xy_ssem.at[3, d], xy_rsem.at[3, d], x_devices[d])
        )
    for copy in dw_copies:
        copy.wait()
    dw_line = dw_xy[0]
    for slot in range(1, BLOCKS):
        dw_line = dw_line + dw_xy[slot]
    dw_send[...] = dw_line
    owner = group
    is_owner = z == owner
    toward = lax.rem(owner - z + CHIPS_Z, CHIPS_Z)
    away = lax.rem(z - owner + CHIPS_Z, CHIPS_Z)
    dw_copy = pltpu.make_async_remote_copy(
        src_ref=dw_send, dst_ref=dw_in.at[z], send_sem=dw_ssem.at[0], recv_sem=dw_rsem.at[0, toward],
        device_id=device(core, owner, x, y), device_id_type=MESH,
    )
    pl.when(jnp.logical_not(is_owner))(dw_copy.start)

    @pl.when(is_owner)
    def _():
        dw_in[z] = dw_send[...]

    for copy in copies:
        copy.wait()
    top2 = top1[y] + top_in2[1] + top_in2[2] + top_in2[3]
    low2 = low1[x] + low_in2[1] + low_in2[2] + low_in2[3]
    for tile in range(CHIPS_Z):
        at = TILE * tile
        z_send[tile] = top2[at : at + TILE] if at < SPLIT else low2[at - SPLIT : at - SPLIT + TILE]

    order = [8, 7, 9, 6, 10, 5, 11, 4, 12, 3, 13, 2, 14, 1, 15]
    copies = []
    for d in order:
        copies.append(
            start_remote(z_send.at[z_peers[d]], z_in.at[z], z_ssem.at[0, d], z_rsem.at[0, d], z_devices[d])
        )
    z_in[z] = z_send[z]
    halo_pass_on(halo)
    def dw_spread(d):
        return pltpu.make_async_remote_copy(
            src_ref=dw_sum_ref, dst_ref=dw_done, send_sem=dw_ssem.at[d], recv_sem=dw_rsem.at[1, d],
            device_id=z_devices[d], device_id_type=MESH,
        )

    @pl.when(is_owner)
    def _():
        for d in range(1, CHIPS_Z):
            pltpu.make_async_remote_copy(
                src_ref=dw_send, dst_ref=dw_in.at[z], send_sem=dw_ssem.at[0],
                recv_sem=dw_rsem.at[0, d], device_id=partner, device_id_type=MESH,
            ).wait_recv()
        dw_total = dw_in[0]
        for tile in range(1, CHIPS_Z):
            dw_total = dw_total + dw_in[tile]
        dw_sum_ref[...] = dw_total
        for d in order:
            dw_spread(d).start()
        dw_done[...] = dw_total

    for copy in copies:
        copy.wait()
    total = z_in[0]
    for tile in range(1, CHIPS_Z):
        total = total + z_in[tile]
    z_own[...] = total

    copies = []
    for d in order:
        copies.append(
            start_remote(z_own, z_all.at[z], z_ssem.at[1, d], z_rsem.at[1, d], z_devices[d])
        )
    z_all[z] = z_own[...]
    halo_wait(halo)
    fill_padded(padded2, edge_rows, grad_block, low2h, high2h, left2h, right2h)

    def finish(n, b, row, total):
        cells = pl.ds(pl.multiple_of(n * cols, cols), cols)
        out_grad_ref[b, row] = (misfit[cells] + total).astype(bf16)

    run_stencil(padded2, weight, shape, True, finish)

    @pl.when(is_owner)
    def _():
        for d in range(1, CHIPS_Z):
            dw_spread(d).wait_send()

    @pl.when(jnp.logical_not(is_owner))
    def _():
        dw_copy.wait_send()
        pltpu.make_async_remote_copy(
            src_ref=dw_sum_ref, dst_ref=dw_done, send_sem=dw_ssem.at[0],
            recv_sem=dw_rsem.at[1, away], device_id=partner, device_id_type=MESH,
        ).wait_recv()

    for copy in copies:
        copy.wait()
    tiles = z_all[...].reshape(SIDE, SIDE)
    dw_tile = jnp.concatenate(
        [dw_done[...], jnp.zeros((DW_PAD - TILE, SIDE), jnp.float32)], axis=0
    )
    top_g1[y] = tiles[:SPLIT].astype(jnp.bfloat16)
    low_g1[x] = jnp.concatenate([tiles[SPLIT:], dw_tile], axis=0).astype(jnp.bfloat16)

    copies = []
    for d in (2, 1, 3):
        copies.append(
            start_remote(top_g1.at[y], top_g1.at[y], xy_ssem.at[4, d], xy_rsem.at[4, d], y_devices[d])
        )
        copies.append(
            start_remote(low_g1.at[x], low_g1.at[x], xy_ssem.at[5, d], xy_rsem.at[5, d], x_devices[d])
        )
    for copy in copies:
        copy.wait()

    copies = []
    for d in (2, 1, 3):
        copies.append(
            start_remote(top_g1, top_all.at[core, x], xy_ssem.at[6, d], xy_rsem.at[6, d], x_devices[d])
        )
        copies.append(
            start_remote(low_g1, low_all.at[core, y], xy_ssem.at[7, d], xy_rsem.at[7, d], y_devices[d])
        )
    top_all[core, x] = top_g1[...]
    low_all[core, y] = low_g1[...]
    core_copies = []

    def to_partner(buffer, slot, k, part):
        core_copies.append(
            start_remote(
                buffer.at[core, slot], buffer.at[core, slot], pair_ssem.at[part, k],
                pair_rsem.at[part, k], partner,
            )
        )

    to_partner(top_all, x, 0, 0)
    to_partner(low_all, y, 0, 1)
    for k, d in ((2, 1), (3, 1), (4, 3), (5, 3), (0, 2), (1, 2)):
        copies[k].wait_recv()
        if k % 2 == 0:
            to_partner(top_all, lax.rem(x - d + 4, 4), d, 0)
        else:
            to_partner(low_all, lax.rem(y - d + 4, 4), d, 1)
    for copy in copies:
        copy.wait_send()
    for copy in core_copies:
        copy.wait()
    for which, out in enumerate((out_a, out_b)):
        for block in range(BLOCKS):
            bx, by = block // 4, block % 4
            across_blocks = 8 if which == 0 else 2
            row, col = SIDE * (block // across_blocks), SIDE * (block % across_blocks)
            out[row : row + SPLIT, col : col + SIDE] = top_all[which, bx, by]
            out[row + SPLIT : row + SIDE, col : col + SIDE] = low_all[which, by, bx, : SIDE - SPLIT]
            p, q = block // 2, DW_ROWS * (block % 2)
            size = weight.shape[0]
            if p < size:
                dw_rows = low_all[which, by, bx, REST:].astype(f32)[: min(DW_ROWS, size - q)]
                out_dw[p, q : q + dw_rows.shape[0], which * SIDE : (which + 1) * SIDE] = (
                    dw_rows / cell_total
                )


def whole_step(block, sent, weight, gain, w_in, w_out, scale):
    f32, bf16 = jnp.float32, jnp.bfloat16
    batch, rows, cols, channels = block.shape
    cells, lats = batch * rows * cols, sent.shape[1] // rows
    edge_cells = batch * rows * WIDTH
    vmem = pl.BlockSpec(memory_space=pltpu.VMEM)
    across = pltpu.VMEM((batch, WIDTH, cols, channels), bf16)
    along = pltpu.VMEM((3, edge_cells, channels), bf16)
    padded = pltpu.VMEM((batch, rows + 2 * WIDTH, cols + 2 * WIDTH + 2, channels), f32)
    dw_shape = (2, BLOCKS * DW_ROWS, SIDE)
    cell_f32 = pltpu.VMEM((cells, channels), f32)
    return pl.pallas_call(
        step_kernel,
        out_shape=(
            jax.ShapeDtypeStruct(w_in.shape, bf16),
            jax.ShapeDtypeStruct(w_out.shape, bf16),
            jax.ShapeDtypeStruct(weight.shape, f32),
            jax.ShapeDtypeStruct(block.shape, bf16),
        ),
        in_specs=[vmem] * 7,
        out_specs=(vmem,) * 4,
        scratch_shapes=[
            pltpu.VMEM((2, edge_cells, channels), f32),
            pltpu.VMEM((2, edge_cells, channels), bf16),
            across,
            across,
            along,
            along,
            pltpu.VMEM((2, 3, edge_cells, channels), f32),
            padded,
            pltpu.VMEM((lats, batch, rows, sent.shape[2], channels), bf16),
            pltpu.VMEM((lats, batch * rows, sent.shape[2], channels), f32),
            cell_f32,
            cell_f32,
            cell_f32,
            pltpu.VMEM((cells, w_in.shape[1]), bf16),
            pltpu.VMEM((cells, w_in.shape[1]), f32),
            cell_f32,
            cell_f32,
            pltpu.VMEM(block.shape, bf16),
            pltpu.VMEM((2, edge_cells, channels), bf16),
            across,
            across,
            along,
            along,
            padded,
            pltpu.VMEM(dw_shape, f32),
            pltpu.VMEM((2, BLOCKS, SIDE, SIDE), f32),
            pltpu.VMEM((BLOCKS, SIDE, SIDE), f32),
            pltpu.VMEM(dw_shape[1:], f32),
            pltpu.VMEM((4, 4, SPLIT, SIDE), f32),
            pltpu.VMEM((4, 4, REST, SIDE), f32),
            pltpu.VMEM((4, 4, SPLIT, SIDE), bf16),
            pltpu.VMEM((4, 4, REST, SIDE), bf16),
            pltpu.VMEM((4, 4, SPLIT, SIDE), bf16),
            pltpu.VMEM((4, 4, REST, SIDE), bf16),
            pltpu.VMEM((4, SPLIT, SIDE), f32),
            pltpu.VMEM((4, REST, SIDE), f32),
            pltpu.VMEM((4, SPLIT, SIDE), f32),
            pltpu.VMEM((4, REST, SIDE), f32),
            pltpu.VMEM((CHIPS_Z, TILE, SIDE), f32),
            pltpu.VMEM((CHIPS_Z, TILE, SIDE), f32),
            pltpu.VMEM((TILE, SIDE), f32),
            pltpu.VMEM((CHIPS_Z, TILE, SIDE), f32),
            pltpu.VMEM((TILE, SIDE), f32),
            pltpu.VMEM((CHIPS_Z, TILE, SIDE), f32),
            pltpu.VMEM((TILE, SIDE), f32),
            pltpu.VMEM((TILE, SIDE), f32),
            pltpu.VMEM((BLOCKS, TILE, SIDE), f32),
            pltpu.VMEM((BLOCKS, TILE, SIDE), f32),
            pltpu.VMEM((4, SPLIT, SIDE), bf16),
            pltpu.VMEM((4, LOWER, SIDE), bf16),
            pltpu.VMEM((2, 4, 4, SPLIT, SIDE), bf16),
            pltpu.VMEM((2, 4, 4, LOWER, SIDE), bf16),
            pltpu.SemaphoreType.DMA((4,)),
            pltpu.SemaphoreType.DMA((4,)),
            pltpu.SemaphoreType.DMA((8, 4)),
            pltpu.SemaphoreType.DMA((8, 4)),
            pltpu.SemaphoreType.DMA((2, CHIPS_Z)),
            pltpu.SemaphoreType.DMA((2, CHIPS_Z)),
            pltpu.SemaphoreType.DMA((8,)),
            pltpu.SemaphoreType.DMA((8,)),
            pltpu.SemaphoreType.DMA((8,)),
            pltpu.SemaphoreType.DMA((8,)),
            pltpu.SemaphoreType.DMA((lats,)),
            pltpu.SemaphoreType.DMA((lats,)),
            pltpu.SemaphoreType.DMA,
            pltpu.SemaphoreType.DMA((CHIPS_Z,)),
            pltpu.SemaphoreType.DMA((2, CHIPS_Z)),
            pltpu.SemaphoreType.DMA((BLOCKS,)),
            pltpu.SemaphoreType.DMA((BLOCKS,)),
            pltpu.SemaphoreType.DMA((2, 4)),
            pltpu.SemaphoreType.DMA((2, 4)),
        ],
        compiler_params=pltpu.CompilerParams(collective_id=0, has_side_effects=True),
    )(block, sent, weight, gain, w_in, w_out, scale)


def local(student, teacher, dw_weight, norm_gain, w_in, w_out, layer_scale):
    batch_size, tile_rows, tile_cols, channel_count = student.shape
    lats = lax.axis_size("lat")
    cell_total = batch_size * tile_rows * lats * tile_cols * lax.axis_size("lon")
    sum_in, sum_out, sum_dw, grad_student = whole_step(
        student, teacher, dw_weight, norm_gain[None], w_in, w_out, layer_scale[None]
    )
    return (
        grad_student,
        sum_in.astype(jnp.float32) / cell_total,
        sum_out.astype(jnp.float32) / cell_total,
        sum_dw,
    )


def solution(mesh):
    placed = (
        P(None, "lat", "lon", None),
        P(None, None, ("lon", "lat"), None),
        P(),
        P(),
        P(),
        P(),
        P(),
    )
    return jax.shard_map(
        local,
        mesh=mesh,
        in_specs=placed,
        out_specs=(P(None, "lat", "lon", None), P(), P(), P()),
        check_vma=False,
    )
```

```python
import jax
import jax.numpy as jnp
from jax import lax
from jax.experimental import pallas as pl
from jax.experimental.pallas import tpu as pltpu
from jax.sharding import PartitionSpec as P

slope_coef = 0.7978845608028654
cubic_coef = 0.044715
norm_eps = 1e-06
MESH = pl.DeviceIdType.MESH

def start_remote(source, target, ssem, rsem, device_to):
    copy = pltpu.make_async_remote_copy(
        src_ref=source, dst_ref=target, send_sem=ssem, recv_sem=rsem,
        device_id=device_to, device_id_type=MESH,
    )
    copy.start()
    return copy


WIDTH = 3


def halo_friends(lat, lon, lats, lons):
    steps = [(0, 1), (0, -1), (1, 0), (-1, 0)]
    return [
        {"lat": lax.rem(lat + dl + lats, lats), "lon": lax.rem(lon + dn + lons, lons)}
        for dl, dn in steps
    ]


def halo_copies(block, edges, low, high, left, right, ssem, rsem):
    lats, lons = lax.axis_size("lat"), lax.axis_size("lon")
    lat, lon = lax.axis_index("lat"), lax.axis_index("lon")
    rows = block.shape[1]
    up = {"lat": jnp.minimum(lat + 1, lats - 1), "lon": lon}
    down = {"lat": jnp.maximum(lat - 1, 0), "lon": lon}
    first = lat == 0
    last = lat == lats - 1
    inner_up, inner_down = jnp.logical_not(last), jnp.logical_not(first)
    plan = [
        (edges.at[1], left.at[1], {"lat": lat, "lon": lax.rem(lon + 1, lons)}, None, None),
        (edges.at[0], right.at[1], {"lat": lat, "lon": lax.rem(lon + lons - 1, lons)}, None, None),
        (block.at[:, pl.ds(rows - WIDTH, WIDTH)], low, up, inner_up, inner_down),
        (block.at[:, pl.ds(0, WIDTH)], high, down, inner_down, inner_up),
        (left.at[1], left.at[0], up, inner_up, inner_down),
        (right.at[1], right.at[0], up, inner_up, inner_down),
        (left.at[1], left.at[2], down, inner_down, inner_up),
        (right.at[1], right.at[2], down, inner_down, inner_up),
    ]
    copies = []
    for k, (source, target, device_to, sends, comes) in enumerate(plan):
        copy = pltpu.make_async_remote_copy(
            src_ref=source, dst_ref=target, send_sem=ssem.at[k], recv_sem=rsem.at[k],
            device_id=device_to, device_id_type=MESH,
        )
        copies.append((copy, sends, comes))
    return copies


def run_if(condition, action):
    if condition is None:
        action()
    else:
        pl.when(condition)(action)


def halo_start(copies, low, high, left, right):
    lats, lat = lax.axis_size("lat"), lax.axis_index("lat")
    for copy, sends, _ in copies[:4]:
        run_if(sends, copy.start)

    @pl.when(lat == 0)
    def _():
        low[...] = jnp.zeros_like(low)
        left[0] = jnp.zeros(left.shape[1:], left.dtype)
        right[0] = jnp.zeros(right.shape[1:], right.dtype)

    @pl.when(lat == lats - 1)
    def _():
        high[...] = jnp.zeros_like(high)
        left[2] = jnp.zeros(left.shape[1:], left.dtype)
        right[2] = jnp.zeros(right.shape[1:], right.dtype)


def halo_pass_on(copies):
    for copy, _, _ in copies[:2]:
        copy.wait_recv()
    for copy, sends, _ in copies[4:]:
        run_if(sends, copy.start)


def halo_wait(copies):
    for k, (copy, sends, comes) in enumerate(copies):
        run_if(sends, copy.wait_send)
        if k >= 2:
            run_if(comes, copy.wait_recv)


def pack_edges(block, rows_f32, edges):
    batch, rows, cols, channels = block.shape
    for b in range(batch):
        for row in range(rows):
            at = (b * rows + row) * WIDTH
            line = block[b, row].astype(jnp.float32)
            rows_f32[0, at : at + WIDTH] = line[:WIDTH]
            rows_f32[1, at : at + WIDTH] = line[cols - WIDTH :]
    edges[...] = rows_f32[...].astype(edges.dtype)


def fill_padded(padded, edge_rows, block, low, high, left, right):
    batch, rows, cols, channels = block.shape
    for side, ref in enumerate((left, right)):
        for k in range(3):
            edge_rows[side, k] = ref[k].astype(jnp.float32)
    for b in range(batch):
        for row in range(rows + 2 * WIDTH):
            if row < WIDTH:
                line, k, r = low[b, row], 0, rows - WIDTH + row
            elif row < WIDTH + rows:
                line, k, r = block[b, row - WIDTH], 1, row - WIDTH
            else:
                line, k, r = high[b, row - WIDTH - rows], 2, row - WIDTH - rows
            at = (b * rows + r) * WIDTH
            padded[b, row, WIDTH : WIDTH + cols] = line.astype(jnp.float32)
            padded[b, row, :WIDTH] = edge_rows[0, k, at : at + WIDTH]
            padded[b, row, WIDTH + cols : 2 * WIDTH + cols] = edge_rows[1, k, at : at + WIDTH]


def run_stencil(padded, weight, shape, flipped, emit):
    batch, rows, cols, channels = shape
    size = weight.shape[0]

    @pl.loop(0, batch * rows)
    def _(n):
        b, row = n // rows, lax.rem(n, rows)
        total = jnp.zeros((cols, channels), jnp.float32)
        for p in range(size):
            for q in range(size):
                row_at = size - 1 - p if flipped else p
                col_at = size - 1 - q if flipped else q
                total = total + weight[p, q : q + 1] * padded[b, row + row_at, col_at : col_at + cols]
        emit(n, b, row, total)


def tap_sums(padded, cell_grad, shape, size, dw):
    batch, rows, cols, channels = shape
    dw[...] = jnp.zeros_like(dw)

    @pl.loop(0, size)
    def _(p):
        for q in range(size):
            total = jnp.zeros((TILE, channels), jnp.float32)
            for n in range(batch * rows):
                b, row = n // rows, n % rows
                product = padded[b, row + p, q : q + cols] * cell_grad[n * cols : (n + 1) * cols]
                for t in range(cols // TILE):
                    total = total + product[t * TILE : (t + 1) * TILE]
            line = jnp.sum(total, axis=0, keepdims=True)
            for half in range(2):
                dw[half, pl.ds(p * TILE + q, 1)] = line[:, half * SIDE : (half + 1) * SIDE]


BLOCKS, SIDE, SPLIT, TILE, DW_ROWS, DW_PAD = 16, 128, 64, 8, 4, 16
REST = SIDE - SPLIT
LOWER = REST + DW_PAD
CHIPS_Z = 16
CHUNK = 256


def block_slot(which, row, col):
    return row * 8 + col if which == 0 else row * 2 + col


def step_kernel(
    block, sent, weight, gain, w_in, w_out, scale,
    out_a, out_b, out_dw, out_grad_ref,
    edge_f32, edges, low, high, left, right, edge_rows, padded, came, came_f32, target,
    smoothed, unit, hid, slope, misfit, cell_grad, grad_block,
    edges2, low2h, high2h, left2h, right2h, padded2, dw_ref,
    own, other, dw_other, top, low_part, top_b, low_b, top_in1, low_in1, top1, low1, top1_b, low1_b, top_in2, low_in2,
    z_send, z_in, z_own, z_all, dw_send, dw_in, dw_sum_ref, dw_done, dw_parts, dw_xy, top_g1, low_g1, top_all, low_all,
    core_ssem, core_rsem, xy_ssem, xy_rsem, z_ssem, z_rsem, halo_ssem, halo_rsem,
    halo2_ssem, halo2_rsem, teach_ssem, teach_rsem, local_sem, dw_ssem, dw_rsem, dw_xy_ssem, dw_xy_rsem, pair_ssem, pair_rsem,
):
    f32, bf16 = jnp.float32, jnp.bfloat16
    lats, lons = lax.axis_size("lat"), lax.axis_size("lon")
    cell_total = block.shape[0] * block.shape[1] * block.shape[2] * lats * lons
    lat, lon = lax.axis_index("lat"), lax.axis_index("lon")
    core = lax.rem(lat, 2)
    z = lax.rem(lon, 2) * 8 + lat // 2
    x = lon // 8
    y = lax.rem(lon // 2, 4)

    def device(core_to, z_to, x_to, y_to):
        return {
            "lat": lax.rem(z_to, 8) * 2 + core_to,
            "lon": x_to * 8 + y_to * 2 + z_to // 8,
        }

    partner = device(1 - core, z, x, y)
    x_peers = [lax.rem(x + d, 4) for d in range(4)]
    y_peers = [lax.rem(y + d, 4) for d in range(4)]
    z_peers = [lax.rem(z + d, CHIPS_Z) for d in range(CHIPS_Z)]
    x_devices = [device(core, z, p, y) for p in x_peers]
    y_devices = [device(core, z, x, p) for p in y_peers]
    z_devices = [device(core, p, x, y) for p in z_peers]

    barrier = pltpu.get_barrier_semaphore()
    friends = [partner] + x_devices[1:] + y_devices[1:] + z_devices[1:]
    diagonal = [(dx, dy) for dx in range(1, 4) for dy in range(1, 4)]
    friends = friends + [device(core, z, x_peers[dx], y_peers[dy]) for dx, dy in diagonal]
    lat_peers = [lax.rem(lat + d, lats) for d in range(lats)]
    friends = friends + halo_friends(lat, lon, lats, lons)[:2]
    friends = friends + [{"lat": p, "lon": lon} for p in lat_peers[1:]]
    for friend in friends:
        pl.semaphore_signal(barrier, inc=1, device_id=friend, device_id_type=MESH)

    mine = pltpu.make_async_copy(sent.at[:, pl.ds(lat * block.shape[1], block.shape[1])], came.at[lat], local_sem)
    mine.start()
    pack_edges(block, edge_f32, edges)
    pl.semaphore_wait(barrier, len(friends))

    front = halo_copies(block, edges, low, high, left, right, halo_ssem, halo_rsem)
    halo_start(front, low, high, left, right)
    teaching = [
        start_remote(
            sent.at[:, pl.ds(lat_peers[d] * block.shape[1], block.shape[1])], came.at[lat], teach_ssem.at[d], teach_rsem.at[d],
            {"lat": lat_peers[d], "lon": lon},
        )
        for d in range(1, lats)
    ]
    halo_pass_on(front)
    halo_wait(front)
    fill_padded(padded, edge_rows, block, low, high, left, right)

    shape = block.shape
    batch, rows, cols, channels = shape

    def keep(n, b, row, total):
        smoothed[pl.ds(pl.multiple_of(n * cols, cols), cols)] = total

    run_stencil(padded, weight, shape, False, keep)
    smooth = smoothed[...]
    average = jnp.mean(smooth, axis=-1, keepdims=True)
    centred = smooth - average
    variance = jnp.mean(centred * centred, axis=-1, keepdims=True)
    inv_std = lax.rsqrt(variance + norm_eps)
    unit[...] = centred * inv_std
    normed = (unit[...] * gain[...]).astype(bf16)
    mlp_out = jnp.zeros((batch * rows * cols, channels), f32)
    hidden_size = w_in.shape[1]
    for at in range(0, hidden_size, CHUNK):
        preact = jnp.dot(normed, w_in[:, at : at + CHUNK], preferred_element_type=f32)
        tangent = jnp.tanh(slope_coef * (preact + cubic_coef * preact * preact * preact))
        hidden = (0.5 * preact * (1.0 + tangent)).astype(bf16)
        hid[:, at : at + CHUNK] = hidden
        slope[:, at : at + CHUNK] = 0.5 * (1.0 + tangent) + 0.5 * preact * (
            1.0 - tangent * tangent
        ) * slope_coef * (1.0 + 3.0 * cubic_coef * preact * preact)
        mlp_out = mlp_out + jnp.dot(hidden, w_out[at : at + CHUNK], preferred_element_type=f32)

    mine.wait()
    for copy in teaching:
        copy.wait()
    for src in range(lats):
        for n in range(batch * rows):
            came_f32[src, n] = came[src, n // rows, n % rows].astype(f32)
    part = cols // lats
    for src in range(lats):
        for n in range(batch * rows):
            at = n * cols + src * part
            target[at : at + part] = came_f32[src, n]
    student = jnp.concatenate(
        [block[n // rows, n % rows] for n in range(batch * rows)], axis=0
    ).astype(f32)
    misfit[...] = (student + scale[...] * mlp_out) - target[...]
    out_grad = (scale[...] * misfit[...]).astype(bf16)
    contract_cells = (((0,), (0,)), ((), ()))
    contract_last = (((1,), (1,)), ((), ()))

    def keep_product(which, row_at, col_at, product):
        for row in range(product.shape[0] // SIDE):
            for col in range(product.shape[1] // SIDE):
                slot = block_slot(which, row_at // SIDE + row, col_at // SIDE + col)
                own[which, slot] = product[
                    row * SIDE : (row + 1) * SIDE, col * SIDE : (col + 1) * SIDE
                ]

    normed_grad = jnp.zeros((batch * rows * cols, channels), f32)
    for at in range(0, hidden_size, CHUNK):
        hidden_grad = lax.dot_general(
            out_grad, w_out[at : at + CHUNK], contract_last, preferred_element_type=f32
        )
        preact_grad = (hidden_grad * slope[:, at : at + CHUNK]).astype(bf16)
        keep_product(
            0, 0, at, lax.dot_general(normed, preact_grad, contract_cells, preferred_element_type=f32)
        )
        keep_product(
            1,
            at,
            0,
            lax.dot_general(
                hid[:, at : at + CHUNK], out_grad, contract_cells, preferred_element_type=f32
            ),
        )
        normed_grad = normed_grad + lax.dot_general(
            preact_grad, w_in[:, at : at + CHUNK], contract_last, preferred_element_type=f32
        )
    core_copies = [
        start_remote(own.at[1 - core], other, core_ssem.at[0], core_rsem.at[0], partner)
    ]
    unit_grad = normed_grad * gain[...]
    unit_norm = unit[...]
    first_mean = jnp.mean(unit_grad, axis=-1, keepdims=True)
    second_mean = jnp.mean(unit_grad * unit_norm, axis=-1, keepdims=True)
    conv_grad = (inv_std * (unit_grad - first_mean - unit_norm * second_mean)).astype(bf16)
    for n in range(batch * rows):
        grad_block[n // rows, n % rows] = conv_grad[n * cols : (n + 1) * cols]
    cell_grad[...] = conv_grad.astype(f32)
    pack_edges(grad_block, edge_f32, edges2)
    halo = halo_copies(
        grad_block, edges2, low2h, high2h, left2h, right2h, halo2_ssem, halo2_rsem
    )
    halo_start(halo, low2h, high2h, left2h, right2h)
    tap_sums(padded, cell_grad, shape, weight.shape[0], dw_ref)
    dw_core = start_remote(
        dw_ref.at[1 - core], dw_other, core_ssem.at[1], core_rsem.at[1], partner
    )
    for copy in core_copies:
        copy.wait()
    for block in range(BLOCKS):
        bx, by = block // 4, block % 4
        top[bx, by] = own[core, block, :SPLIT] + other[block, :SPLIT]
        low_part[by, bx] = own[core, block, SPLIT:] + other[block, SPLIT:]

    for k in range(4):
        top_b[k] = top[k].astype(bf16)
        low_b[k] = low_part[k].astype(bf16)
    copies = []
    for d in (2, 1, 3):
        copies.append(
            start_remote(top_b.at[x_peers[d]], top_in1.at[d], xy_ssem.at[0, d], xy_rsem.at[0, d], x_devices[d])
        )
        copies.append(
            start_remote(low_b.at[y_peers[d]], low_in1.at[d], xy_ssem.at[1, d], xy_rsem.at[1, d], y_devices[d])
        )
    dw_core.wait()
    group = x * 4 + y
    for slot in range(BLOCKS):
        lines = slice(DW_ROWS * slot, DW_ROWS * (slot + 1))
        dw_parts[slot, :DW_ROWS] = dw_ref[core, lines] + dw_other[lines]
        dw_parts[slot, DW_ROWS:] = jnp.zeros((TILE - DW_ROWS, SIDE), f32)
    dw_copies = []
    for k in range(1, BLOCKS):
        px, py = x_peers[k // 4], y_peers[k % 4]
        dw_copies.append(
            start_remote(
                dw_parts.at[px * 4 + py], dw_xy.at[group], dw_xy_ssem.at[k], dw_xy_rsem.at[k],
                device(core, z, px, py),
            )
        )
    dw_xy[group] = dw_parts[group]
    for copy in copies:
        copy.wait()
    top1[...] = top[x] + top_in1[1].astype(f32) + top_in1[2].astype(f32) + top_in1[3].astype(f32)
    low1[...] = (
        low_part[y] + low_in1[1].astype(f32) + low_in1[2].astype(f32) + low_in1[3].astype(f32)
    )

    top1_b[...] = top1[...].astype(bf16)
    low1_b[...] = low1[...].astype(bf16)
    copies = []
    for d in (2, 1, 3):
        copies.append(
            start_remote(top1_b.at[y_peers[d]], top_in2.at[d], xy_ssem.at[2, d], xy_rsem.at[2, d], y_devices[d])
        )
        copies.append(
            start_remote(low1_b.at[x_peers[d]], low_in2.at[d], xy_ssem.at[3, d], xy_rsem.at[3, d], x_devices[d])
        )
    for copy in dw_copies:
        copy.wait()
    dw_line = dw_xy[0]
    for slot in range(1, BLOCKS):
        dw_line = dw_line + dw_xy[slot]
    dw_send[...] = dw_line
    owner = group
    is_owner = z == owner
    toward = lax.rem(owner - z + CHIPS_Z, CHIPS_Z)
    away = lax.rem(z - owner + CHIPS_Z, CHIPS_Z)
    dw_copy = pltpu.make_async_remote_copy(
        src_ref=dw_send, dst_ref=dw_in.at[z], send_sem=dw_ssem.at[0], recv_sem=dw_rsem.at[0, toward],
        device_id=device(core, owner, x, y), device_id_type=MESH,
    )
    pl.when(jnp.logical_not(is_owner))(dw_copy.start)

    @pl.when(is_owner)
    def _():
        dw_in[z] = dw_send[...]

    for copy in copies:
        copy.wait()
    top2 = top1[y] + top_in2[1].astype(f32) + top_in2[2].astype(f32) + top_in2[3].astype(f32)
    low2 = low1[x] + low_in2[1].astype(f32) + low_in2[2].astype(f32) + low_in2[3].astype(f32)
    for tile in range(CHIPS_Z):
        at = TILE * tile
        z_send[tile] = top2[at : at + TILE] if at < SPLIT else low2[at - SPLIT : at - SPLIT + TILE]

    order = [8, 7, 9, 6, 10, 5, 11, 4, 12, 3, 13, 2, 14, 1, 15]
    copies = []
    for d in order:
        copies.append(
            start_remote(z_send.at[z_peers[d]], z_in.at[z], z_ssem.at[0, d], z_rsem.at[0, d], z_devices[d])
        )
    z_in[z] = z_send[z]
    halo_pass_on(halo)
    def dw_spread(d):
        return pltpu.make_async_remote_copy(
            src_ref=dw_sum_ref, dst_ref=dw_done, send_sem=dw_ssem.at[d], recv_sem=dw_rsem.at[1, d],
            device_id=z_devices[d], device_id_type=MESH,
        )

    @pl.when(is_owner)
    def _():
        for d in range(1, CHIPS_Z):
            pltpu.make_async_remote_copy(
                src_ref=dw_send, dst_ref=dw_in.at[z], send_sem=dw_ssem.at[0],
                recv_sem=dw_rsem.at[0, d], device_id=partner, device_id_type=MESH,
            ).wait_recv()
        dw_total = dw_in[0]
        for tile in range(1, CHIPS_Z):
            dw_total = dw_total + dw_in[tile]
        dw_sum_ref[...] = dw_total
        for d in order:
            dw_spread(d).start()
        dw_done[...] = dw_total

    for copy in copies:
        copy.wait()
    total = z_in[0]
    for tile in range(1, CHIPS_Z):
        total = total + z_in[tile]
    z_own[...] = total.astype(bf16)

    copies = []
    for d in order:
        copies.append(
            start_remote(z_own, z_all.at[z], z_ssem.at[1, d], z_rsem.at[1, d], z_devices[d])
        )
    z_all[z] = z_own[...]
    halo_wait(halo)
    fill_padded(padded2, edge_rows, grad_block, low2h, high2h, left2h, right2h)

    def finish(n, b, row, total):
        cells = pl.ds(pl.multiple_of(n * cols, cols), cols)
        out_grad_ref[b, row] = (misfit[cells] + total).astype(bf16)

    run_stencil(padded2, weight, shape, True, finish)

    @pl.when(is_owner)
    def _():
        for d in range(1, CHIPS_Z):
            dw_spread(d).wait_send()

    @pl.when(jnp.logical_not(is_owner))
    def _():
        dw_copy.wait_send()
        pltpu.make_async_remote_copy(
            src_ref=dw_sum_ref, dst_ref=dw_done, send_sem=dw_ssem.at[0],
            recv_sem=dw_rsem.at[1, away], device_id=partner, device_id_type=MESH,
        ).wait_recv()

    for copy in copies:
        copy.wait()
    tiles = z_all[...].astype(f32).reshape(SIDE, SIDE)
    dw_tile = jnp.concatenate(
        [dw_done[...], jnp.zeros((DW_PAD - TILE, SIDE), jnp.float32)], axis=0
    )
    top_g1[y] = tiles[:SPLIT].astype(jnp.bfloat16)
    low_g1[x] = jnp.concatenate([tiles[SPLIT:], dw_tile], axis=0).astype(jnp.bfloat16)

    copies = []
    for d in (2, 1, 3):
        copies.append(
            start_remote(top_g1.at[y], top_g1.at[y], xy_ssem.at[4, d], xy_rsem.at[4, d], y_devices[d])
        )
        copies.append(
            start_remote(low_g1.at[x], low_g1.at[x], xy_ssem.at[5, d], xy_rsem.at[5, d], x_devices[d])
        )
    for copy in copies:
        copy.wait()

    copies = []
    for d in (2, 1, 3):
        copies.append(
            start_remote(top_g1, top_all.at[core, x], xy_ssem.at[6, d], xy_rsem.at[6, d], x_devices[d])
        )
        copies.append(
            start_remote(low_g1, low_all.at[core, y], xy_ssem.at[7, d], xy_rsem.at[7, d], y_devices[d])
        )
    top_all[core, x] = top_g1[...]
    low_all[core, y] = low_g1[...]
    core_copies = []

    def to_partner(buffer, slot, k, part):
        core_copies.append(
            start_remote(
                buffer.at[core, slot], buffer.at[core, slot], pair_ssem.at[part, k],
                pair_rsem.at[part, k], partner,
            )
        )

    to_partner(top_all, x, 0, 0)
    to_partner(low_all, y, 0, 1)
    for k, d in ((2, 1), (3, 1), (4, 3), (5, 3), (0, 2), (1, 2)):
        copies[k].wait_recv()
        if k % 2 == 0:
            to_partner(top_all, lax.rem(x - d + 4, 4), d, 0)
        else:
            to_partner(low_all, lax.rem(y - d + 4, 4), d, 1)
    for copy in copies:
        copy.wait_send()
    for copy in core_copies:
        copy.wait()
    for which, out in enumerate((out_a, out_b)):
        for block in range(BLOCKS):
            bx, by = block // 4, block % 4
            across_blocks = 8 if which == 0 else 2
            row, col = SIDE * (block // across_blocks), SIDE * (block % across_blocks)
            out[row : row + SPLIT, col : col + SIDE] = top_all[which, bx, by]
            out[row + SPLIT : row + SIDE, col : col + SIDE] = low_all[which, by, bx, : SIDE - SPLIT]
            p, q = block // 2, DW_ROWS * (block % 2)
            size = weight.shape[0]
            if p < size:
                dw_rows = low_all[which, by, bx, REST:].astype(f32)[: min(DW_ROWS, size - q)]
                out_dw[p, q : q + dw_rows.shape[0], which * SIDE : (which + 1) * SIDE] = (
                    dw_rows / cell_total
                )


def whole_step(block, sent, weight, gain, w_in, w_out, scale):
    f32, bf16 = jnp.float32, jnp.bfloat16
    batch, rows, cols, channels = block.shape
    cells, lats = batch * rows * cols, sent.shape[1] // rows
    edge_cells = batch * rows * WIDTH
    vmem = pl.BlockSpec(memory_space=pltpu.VMEM)
    across = pltpu.VMEM((batch, WIDTH, cols, channels), bf16)
    along = pltpu.VMEM((3, edge_cells, channels), bf16)
    padded = pltpu.VMEM((batch, rows + 2 * WIDTH, cols + 2 * WIDTH + 2, channels), f32)
    dw_shape = (2, BLOCKS * DW_ROWS, SIDE)
    cell_f32 = pltpu.VMEM((cells, channels), f32)
    return pl.pallas_call(
        step_kernel,
        out_shape=(
            jax.ShapeDtypeStruct(w_in.shape, bf16),
            jax.ShapeDtypeStruct(w_out.shape, bf16),
            jax.ShapeDtypeStruct(weight.shape, f32),
            jax.ShapeDtypeStruct(block.shape, bf16),
        ),
        in_specs=[vmem] * 7,
        out_specs=(vmem,) * 4,
        scratch_shapes=[
            pltpu.VMEM((2, edge_cells, channels), f32),
            pltpu.VMEM((2, edge_cells, channels), bf16),
            across,
            across,
            along,
            along,
            pltpu.VMEM((2, 3, edge_cells, channels), f32),
            padded,
            pltpu.VMEM((lats, batch, rows, sent.shape[2], channels), bf16),
            pltpu.VMEM((lats, batch * rows, sent.shape[2], channels), f32),
            cell_f32,
            cell_f32,
            cell_f32,
            pltpu.VMEM((cells, w_in.shape[1]), bf16),
            pltpu.VMEM((cells, w_in.shape[1]), f32),
            cell_f32,
            cell_f32,
            pltpu.VMEM(block.shape, bf16),
            pltpu.VMEM((2, edge_cells, channels), bf16),
            across,
            across,
            along,
            along,
            padded,
            pltpu.VMEM(dw_shape, f32),
            pltpu.VMEM((2, BLOCKS, SIDE, SIDE), f32),
            pltpu.VMEM((BLOCKS, SIDE, SIDE), f32),
            pltpu.VMEM(dw_shape[1:], f32),
            pltpu.VMEM((4, 4, SPLIT, SIDE), f32),
            pltpu.VMEM((4, 4, REST, SIDE), f32),
            pltpu.VMEM((4, 4, SPLIT, SIDE), bf16),
            pltpu.VMEM((4, 4, REST, SIDE), bf16),
            pltpu.VMEM((4, 4, SPLIT, SIDE), bf16),
            pltpu.VMEM((4, 4, REST, SIDE), bf16),
            pltpu.VMEM((4, SPLIT, SIDE), f32),
            pltpu.VMEM((4, REST, SIDE), f32),
            pltpu.VMEM((4, SPLIT, SIDE), bf16),
            pltpu.VMEM((4, REST, SIDE), bf16),
            pltpu.VMEM((4, SPLIT, SIDE), bf16),
            pltpu.VMEM((4, REST, SIDE), bf16),
            pltpu.VMEM((CHIPS_Z, TILE, SIDE), f32),
            pltpu.VMEM((CHIPS_Z, TILE, SIDE), f32),
            pltpu.VMEM((TILE, SIDE), bf16),
            pltpu.VMEM((CHIPS_Z, TILE, SIDE), bf16),
            pltpu.VMEM((TILE, SIDE), f32),
            pltpu.VMEM((CHIPS_Z, TILE, SIDE), f32),
            pltpu.VMEM((TILE, SIDE), f32),
            pltpu.VMEM((TILE, SIDE), f32),
            pltpu.VMEM((BLOCKS, TILE, SIDE), f32),
            pltpu.VMEM((BLOCKS, TILE, SIDE), f32),
            pltpu.VMEM((4, SPLIT, SIDE), bf16),
            pltpu.VMEM((4, LOWER, SIDE), bf16),
            pltpu.VMEM((2, 4, 4, SPLIT, SIDE), bf16),
            pltpu.VMEM((2, 4, 4, LOWER, SIDE), bf16),
            pltpu.SemaphoreType.DMA((4,)),
            pltpu.SemaphoreType.DMA((4,)),
            pltpu.SemaphoreType.DMA((8, 4)),
            pltpu.SemaphoreType.DMA((8, 4)),
            pltpu.SemaphoreType.DMA((2, CHIPS_Z)),
            pltpu.SemaphoreType.DMA((2, CHIPS_Z)),
            pltpu.SemaphoreType.DMA((8,)),
            pltpu.SemaphoreType.DMA((8,)),
            pltpu.SemaphoreType.DMA((8,)),
            pltpu.SemaphoreType.DMA((8,)),
            pltpu.SemaphoreType.DMA((lats,)),
            pltpu.SemaphoreType.DMA((lats,)),
            pltpu.SemaphoreType.DMA,
            pltpu.SemaphoreType.DMA((CHIPS_Z,)),
            pltpu.SemaphoreType.DMA((2, CHIPS_Z)),
            pltpu.SemaphoreType.DMA((BLOCKS,)),
            pltpu.SemaphoreType.DMA((BLOCKS,)),
            pltpu.SemaphoreType.DMA((2, 4)),
            pltpu.SemaphoreType.DMA((2, 4)),
        ],
        compiler_params=pltpu.CompilerParams(collective_id=0, has_side_effects=True),
    )(block, sent, weight, gain, w_in, w_out, scale)


def local(student, teacher, dw_weight, norm_gain, w_in, w_out, layer_scale):
    batch_size, tile_rows, tile_cols, channel_count = student.shape
    lats = lax.axis_size("lat")
    cell_total = batch_size * tile_rows * lats * tile_cols * lax.axis_size("lon")
    sum_in, sum_out, sum_dw, grad_student = whole_step(
        student, teacher, dw_weight, norm_gain[None], w_in, w_out, layer_scale[None]
    )
    return (
        grad_student,
        sum_in.astype(jnp.float32) / cell_total,
        sum_out.astype(jnp.float32) / cell_total,
        sum_dw,
    )


def solution(mesh):
    placed = (
        P(None, "lat", "lon", None),
        P(None, None, ("lon", "lat"), None),
        P(),
        P(),
        P(),
        P(),
        P(),
    )
    return jax.shard_map(
        local,
        mesh=mesh,
        in_specs=placed,
        out_specs=(P(None, "lat", "lon", None), P(), P(), P()),
        check_vma=False,
    )
```
